512 devices in a mesh: head: 4 (over x), tensor: 16 (over y, z_hi), dp: 8 (over z_lo, core).
Axes of the slice: x: 4, y: 8, z: 8 (z_hi: 2, z_lo: 4; z = z_hi * 4 + z_lo), core: 2. Of those that a mesh axis runs over, the one named last changes fastest.
Arguments:
- trunk_hidden: bfloat16 [384, 5120], P('dp', 'tensor'), may hold values from -60 to 60
- next_embeds: bfloat16 [4, 384, 5120], P('head', 'dp', 'tensor'), may hold values from -6 to 6
- combine_weight: bfloat16 [4, 10240, 5120], P('head', 'dp', 'tensor'), may hold values from -0.0625 to 0.0625
- final_gain: float32 [5120], P('tensor'), may hold values from 0.5 to 1.5
- unembed_weight: bfloat16 [16384, 5120], P('dp', 'tensor'), may hold values from -32 to 32
- target_ids: int32 [4, 384], P('head'), may hold values from 0 to 16383
- loss_scale: float32 [4, 384], P('head'), may hold values from 2 to 32
Outputs:
- trunk_grad: float32 [384, 5120], P('dp', 'tensor')
- embed_grad: float32 [4, 384, 5120], P('head', 'dp', 'tensor')
- combine_grad: float32 [4, 10240, 5120], P('head', 'dp', 'tensor')
- unembed_grad: float32 [8, 4, 512, 5120], P('dp', 'head', None, 'tensor')
The draws below stay inside these ranges and needn't reach their ends.
All inputs are finite; a program needn't handle non-finite values.
Results may differ from the reference program's by a relative error of at most 0.02.
Values may be sent and summed in bfloat16 or wider, within the bound.
A program may use at most 64 MiB of HBM per device.

```python
import math
import jax
import jax.numpy as jnp
import numpy as np
from jax import lax

D = 5120
VOCAB = 16384
TOKENS = 384
HEADS = 4
N_DP = 8


def shared_direction(key):
    return jax.random.normal(jax.random.fold_in(key, 7001), (D,), jnp.float32)


def draw_trunk_hidden(key, part):
    noise = jax.random.normal(jax.random.fold_in(key, 11), (TOKENS, D), jnp.float32)
    values = noise
    chosen = jax.random.randint(jax.random.fold_in(key, 13), (8,), 0, TOKENS)
    direction = shared_direction(key)
    aligned = 6.0 * direction[None, :] + 0.3 * jax.random.normal(jax.random.fold_in(key, 14), (8, D), jnp.float32)
    values = values.at[chosen].set(aligned)
    return jnp.clip(values, -60.0, 60.0).astype(jnp.bfloat16)


def draw_unembed_weight(key, part):
    sigma = 3.0 / math.sqrt(D)
    values = sigma * jnp.clip(jax.random.normal(jax.random.fold_in(key, 24), (VOCAB, D), jnp.float32), -6.0, 6.0)
    direction = shared_direction(key)
    chosen = jax.random.permutation(jax.random.fold_in(key, 22), VOCAB)[:6]
    strength = jnp.array([150.0, 148.0, 260.0, 258.0, 380.0, 378.0], jnp.float32)
    extra = 0.5 / math.sqrt(D) * jax.random.normal(jax.random.fold_in(key, 23), (6, D), jnp.float32)
    aligned = strength[:, None] * direction[None, :] / D + extra
    values = values.at[chosen].set(aligned)
    return jnp.clip(values, -32.0, 32.0).astype(jnp.bfloat16)


def touch_ends(result, rng, low, high):
    shape = result.shape
    spot = [jax.random.randint(jax.random.fold_in(rng, axis), (), 0, shape[axis]) for axis in range(len(shape))]
    result = result.at[tuple(spot)].set(low)
    longest = shape.index(max(shape))
    spot[longest] = (spot[longest] + 1) % shape[longest]
    return result.at[tuple(spot)].set(high)


def shard_levels(stream_key, extent, cuts, least, high):
    factor_of = 1.0
    for axis_at, parts in cuts:
        heights = jax.random.uniform(jax.random.fold_in(jax.random.fold_in(stream_key, 6), axis_at), (parts,), jnp.float32, least / len(cuts), high / len(cuts))
        factor_of = factor_of * jnp.repeat(jnp.exp(heights), extent[axis_at] // parts).reshape((-1,) + (1,) * (len(extent) - 1 - axis_at))
    return factor_of


def rank_table(count, slope):
    portions = [(1 << 20) // math.isqrt(standing ** slope) + 1 for standing in range(1, count + 1)]
    width = 1 + sum(portions) // (1 << 30)
    return np.cumsum(np.array([max(1, weight // width) for weight in portions]))


def ranked(stream_key, shape, number_of, skew):
    table = rank_table(number_of, skew)
    lot = jax.random.randint(jax.random.fold_in(stream_key, 1), shape, 0, int(table[number_of - 1]))
    standing = jnp.searchsorted(jnp.asarray(table, jnp.int32), lot, side="right")
    return jax.random.permutation(jax.random.fold_in(stream_key, 2), number_of)[standing].astype(jnp.int32)


def bell_draw(key, shape, spread, bound, pieces=(), held_as=jnp.bfloat16):
    loudness = shard_levels(key, shape, pieces, -0.22, 0.18) if pieces else 1.0
    values = jax.random.normal(key, shape, jnp.float32) * spread * loudness
    return jnp.minimum(jnp.maximum(values, -bound), bound).astype(held_as)


def setup_inputs(seed: int = 0) -> dict:
    streams_of = jax.random.split(jax.random.key(seed), 8)
    return {
        "trunk_hidden": draw_trunk_hidden(jax.random.fold_in(streams_of[7], 71), 0),
        "next_embeds": bell_draw(streams_of[1], (HEADS, TOKENS, D), 1.0, 6.0, ((0, 4), (1, 8), (2, 16))),
        "combine_weight": bell_draw(streams_of[2], (HEADS, 2 * D, D), (2 * D) ** -0.5, 0.0625, ((0, 4), (1, 8), (2, 16))),
        "final_gain": jnp.clip(1.0 + 0.1 * jax.random.normal(streams_of[3], (D,), jnp.float32), 0.5, 1.5),
        "unembed_weight": draw_unembed_weight(jax.random.fold_in(streams_of[7], 71), 0),
        "target_ids": touch_ends(ranked(streams_of[5], (HEADS, TOKENS), VOCAB, 2), jax.random.fold_in(streams_of[5], 3), 0, VOCAB - 1).astype(jnp.int32),
        "loss_scale": jnp.clip(jnp.exp(math.log(32.0) - 2.7725887 * jax.random.uniform(streams_of[6], (HEADS, TOKENS), jnp.float32) ** shard_levels(streams_of[6], (HEADS, TOKENS), ((0, 4),), -0.2, 0.2)), 2.0, 32.0),
    }


epsilon = 1e-05

def contract_rows(left, right):
    return lax.dot_general(left, right, (((0,), (0,)), ((), ())), preferred_element_type=jnp.float32)

def contract_cols(left, right):
    return lax.dot_general(left, right, (((1,), (1,)), ((), ())), preferred_element_type=jnp.float32)

def reference(trunk_hidden, next_embeds, combine_weight, final_gain, unembed_weight, target_ids, loss_scale):
    trunk_float = trunk_hidden.astype(jnp.float32)
    trunk_scale = lax.rsqrt(lax.optimization_barrier(jnp.sum(trunk_float * trunk_float, axis=1)) / D + epsilon)
    trunk_normed = trunk_float * trunk_scale[:, None]
    vocab_ids = lax.broadcasted_iota(jnp.int32, (1, VOCAB), 1)
    unembed_total = jnp.zeros((VOCAB, D), jnp.float32)
    trunk_total = jnp.zeros((TOKENS, D), jnp.float32)
    embed_list = []
    combine_list = []
    for which_head in range(HEADS):
        embed_float = next_embeds[which_head].astype(jnp.float32)
        embed_scale = lax.rsqrt(lax.optimization_barrier(jnp.sum(embed_float * embed_float, axis=1)) / D + epsilon)
        embed_normed = embed_float * embed_scale[:, None]
        joined = jnp.concatenate([trunk_normed.astype(jnp.bfloat16), embed_normed.astype(jnp.bfloat16)], axis=1)
        mixed = trunk_float + jnp.dot(joined, combine_weight[which_head], preferred_element_type=jnp.float32)
        mixed_scale = lax.rsqrt(lax.optimization_barrier(jnp.sum(mixed * mixed, axis=1)) / D + epsilon)
        mixed_normed = mixed * mixed_scale[:, None]
        normed_out = (mixed_normed * final_gain[None, :]).astype(jnp.bfloat16)
        logits = contract_cols(normed_out, unembed_weight)
        largest = lax.optimization_barrier(jnp.max(logits, axis=1, keepdims=True))
        shifted = jnp.exp(logits - largest)
        probs = shifted / lax.optimization_barrier(jnp.sum(shifted, axis=1, keepdims=True))
        hits = (vocab_ids == target_ids[which_head][:, None]).astype(jnp.float32)
        grad_logits = (loss_scale[which_head][:, None] * (probs - hits)).astype(jnp.bfloat16)
        grad_normed = jnp.dot(grad_logits, unembed_weight, preferred_element_type=jnp.float32)
        vocab_term = lax.optimization_barrier(contract_rows(grad_logits, normed_out).astype(jnp.bfloat16))
        unembed_total = unembed_total + vocab_term.astype(jnp.float32)
        scaled_grad = grad_normed * final_gain[None, :]
        grad_dots = lax.optimization_barrier(jnp.sum(scaled_grad * mixed_normed, axis=1)) / D
        grad_mixed = mixed_scale[:, None] * (scaled_grad - mixed_normed * grad_dots[:, None])
        grad_mixed_low = grad_mixed.astype(jnp.bfloat16)
        combine_list.append(contract_rows(joined, grad_mixed_low))
        joined_grad = contract_cols(grad_mixed_low, combine_weight[which_head])
        trunk_side = joined_grad[:, :D]
        embed_side = joined_grad[:, D:]
        trunk_dots = lax.optimization_barrier(jnp.sum(trunk_side * trunk_normed, axis=1)) / D
        embed_dots = lax.optimization_barrier(jnp.sum(embed_side * embed_normed, axis=1)) / D
        embed_list.append(embed_scale[:, None] * (embed_side - embed_normed * embed_dots[:, None]))
        trunk_total = trunk_total + grad_mixed + trunk_scale[:, None] * (trunk_side - trunk_normed * trunk_dots[:, None])
    unembed_grad = unembed_total.reshape(N_DP, HEADS, VOCAB // (N_DP * HEADS), D)
    return (trunk_total, jnp.stack(embed_list), jnp.stack(combine_list), unembed_grad)
```

```python
import jax
import jax.numpy as jnp
from jax import lax
from jax.experimental import pallas as pl
from jax.experimental.pallas import tpu as pltpu
from jax.sharding import PartitionSpec as P

D = 5120
EPS = 1e-05
R = 48
N = 192
C = 320
CP = 384
V = 2048
VC = 256
MESH = pl.DeviceIdType.MESH
HI = lax.Precision.HIGHEST
f32 = jnp.float32
bf16 = jnp.bfloat16


def dot(left, right, a, b, precision=None):
    return lax.dot_general(
        left, right, (((a,), (b,)), ((), ())), precision=precision, preferred_element_type=f32
    )


def kernel(
    xb, w, u, gain, tgt, wt,
    tg, eg, cg, ug,
    W2, XB, XS, PB, R2, T, Y8, MX, UP, LP, RL, MSC, YN, YS,
    SB0, SY0, SB1, SY1, SB2, SZ2, GA, GS, GN, NB, NR, SG, DCB, DCR, SB3, SY3,
    GMF, GML, GMS, JP, RJ, SD, PRE, XPR, SB4, SY4, SB5, S7, VB, VR, VSB, VSR,
    ssem, rsem, lsem,
):
    h = lax.axis_index("head")
    t = lax.axis_index("tensor")
    d = lax.axis_index("dp")
    y, zh = lax.div(t, 2), lax.rem(t, 2)
    zl, c = lax.div(d, 2), lax.rem(d, 2)
    z = zh * 4 + zl
    oc, ozh = 1 - c, 1 - zh

    def dev(h_=None, y_=None, z_=None, c_=None):
        h_ = h if h_ is None else h_
        y_ = y if y_ is None else y_
        z_ = z if z_ is None else z_
        c_ = c if c_ is None else c_
        return (h_, y_ * 2 + lax.div(z_, 4), lax.rem(z_, 4) * 2 + c_)

    def add(value, step, size):
        return lax.rem(value + (step + size), size)

    sib = dev(c_=oc)
    right, left = dev(y_=add(y, 1, 8)), dev(y_=add(y, -1, 8))
    me = dev()

    counts = {"s": 0, "r": 0}

    def slots(n):
        first = counts["s"]
        counts["s"] += n
        return first

    finals = []

    def copy(src, dst, s, r, to):
        return pltpu.make_async_remote_copy(
            src_ref=src, dst_ref=dst, send_sem=ssem.at[s], recv_sem=rsem.at[r],
            device_id=to, device_id_type=MESH,
        )

    def when(cond, body):
        if cond is None:
            body()
        else:
            pl.when(cond)(body)

    def send(src, dst, s, r, to, cond=None):
        when(cond, lambda: copy(src(), dst(), s, r, to).start())
        finals.append((cond, lambda: copy(src(), dst(), s, r, to).wait_send()))

    def recv(dst, r):
        copy(dst, dst, 0, r, me).wait_recv()

    lane = lax.broadcasted_iota(jnp.int32, (R, CP), 1)
    e8 = (
        lax.broadcasted_iota(jnp.int32, (8, 128), 0) == lax.broadcasted_iota(jnp.int32, (8, 128), 1)
    ).astype(f32)

    def pick(x, at):
        ids = lax.broadcasted_iota(jnp.int32, x.shape, x.ndim - 1)
        return jnp.sum(jnp.where(ids == at, x, 0.0), axis=-1, keepdims=True)

    def to_rows(first, second=None):
        ids = lax.broadcasted_iota(jnp.int32, (first.shape[0], 128), 1)
        v = jnp.where(ids == 0, first, 0.0)
        if second is not None:
            v = jnp.where(ids == 1, second, v)
        return dot(e8, v, 1, 1, HI)

    def to_cols(rows):
        return dot(rows, e8, 0, 0, HI)

    def widen(value, extra):
        T[:, 0:C] = value
        return jnp.where(lane >= C, extra, T[...])

    barrier = pltpu.get_barrier_semaphore()
    peers = [dev(y_=add(y, j, 8)) for j in range(1, 8)]
    peers += [dev(z_=add(z, j, 8)) for j in range(1, 8)]
    peers += [dev(h_=add(h, j, 4)) for j in range(1, 4)]
    peers += [dev(h_=add(h, j, 4), z_=ozh * 4 + zl) for j in range(1, 4)]
    peers += [sib, dev(z_=ozh * 4 + zl, c_=oc)]
    for to in peers:
        pl.semaphore_signal(barrier, inc=1, device_id=to, device_id_type=MESH)
    own_w = pltpu.make_async_copy(w, W2.at[c], lsem.at[0])
    own_w.start()
    T[...] = jnp.zeros_like(T)
    for ref in (SB0, SB1, SB2, SB3, SB4, SB5):
        ref[...] = jnp.zeros_like(ref)
    PB[...] = jnp.zeros_like(PB)
    pl.semaphore_wait(barrier, len(peers))

    yq, ym = lax.div(y, 4), lax.rem(y, 4)
    hf = lax.rem(zl, 2)
    in_half = hf == yq
    a_s, a_r = slots(4), slots(8)
    for kind in range(2):
        for zh_to in range(2):
            z_to = zh_to * 4 + kind * 2 + yq
            send(
                lambda kind=kind: xb.at[kind], lambda: XB.at[ym, z],
                a_s + kind * 2 + zh_to, a_r + z, dev(z_=z_to), z_to != z,
            )

            def keep(kind=kind):
                XB[ym, z] = xb[kind]

            pl.when(z_to == z)(keep)
    w_s = slots(1)
    send(lambda: w, lambda: W2.at[c], w_s, w_s, sib)

    owner = c == zh
    donor = c != zh
    u_q, u_f, u_x, u_d, u_b = slots(4), slots(1), slots(4), slots(1), slots(4)
    own_u = lambda: pltpu.make_async_copy(u, UP.at[zh], lsem.at[1])
    pl.when(owner)(lambda: own_u().start())

    @pl.when(in_half)
    def _():
        for j in range(1, 8):
            zs = add(z, j, 8)
            recv(XB.at[ym, zs], a_r + zs)

    mine = pl.ds(h * 512, 512)
    send(lambda: u.at[mine], lambda: UP.at[zh, mine], u_d, u_q + h, dev(z_=ozh * 4 + zl), donor)

    b_s = slots(16)
    for i in range(8):
        for way in range(2):
            s = add(y, -i, 8) if way == 0 else add(y, i, 8)
            k = lax.rem(s, 4)
            cond = lax.div(s, 4) == hf
            for unit in range(2):
                part = pl.ds(way * 4 + unit * 2, 2)
                idx = b_s + (way * 4 + k) * 2 + unit
                if i > 0:
                    pl.when(cond)(lambda: recv(XB.at[k, part], idx))
                if i < 7:
                    send(
                        lambda k=k, part=part: XB.at[k, part], lambda k=k, part=part: XB.at[k, part],
                        idx, idx, right if way == 0 else left, cond,
                    )

    send(lambda: u, lambda: UP.at[zh], u_f, u_f, sib, owner)
    pl.when(owner)(lambda: recv(UP.at[ozh, mine], u_q + h))
    for j in range(1, 4):
        send(
            lambda: UP.at[ozh, mine], lambda: UP.at[ozh, mine], u_x + j, u_q + h,
            dev(h_=add(h, j, 4)), owner,
        )
    send(lambda: UP.at[ozh, mine], lambda: UP.at[ozh, mine], u_b, u_q + h, sib, owner)

    own_w.wait()
    recv(W2.at[oc], w_s)
    acc = jnp.zeros((N, C), f32)
    squares = jnp.zeros((N, 1), f32)
    for q in range(8):
        block = XB[q // 2, (q % 2) * 4 : (q % 2) * 4 + 4].reshape(N, C)
        acc = acc + dot(block, W2[q // 4, (q % 4) * C : (q % 4 + 1) * C, :], 1, 0)
        wide = block.astype(f32)
        squares = squares + jnp.sum(wide * wide, axis=1, keepdims=True)
    PB[:, :, 0:C] = acc.reshape(4, R, C)
    lane3 = lax.broadcasted_iota(jnp.int32, (4, R, CP), 2)
    PB[...] = jnp.where(lane3 >= C, squares.reshape(4, R, 1), PB[...])
    p_s, p_r = slots(4), slots(4)
    for j in range(1, 4):
        zt = add(zl, j, 4)
        send(
            lambda zt=zt: PB.at[zt], lambda: R2.at[zl], p_s + j, p_r + zl, dev(z_=zh * 4 + zt)
        )
    R2[zl] = PB[zl]
    x_s = slots(1)
    send(lambda: XB.at[pl.ds(2 * oc, 2)], lambda: XS, x_s, x_s, sib)
    for j in range(1, 4):
        zt = add(zl, j, 4)
        recv(R2.at[zt], p_r + zt)
    from_trunk = R2[0] + R2[1]
    from_embed = R2[2] + R2[3]
    trunk = xb[0].astype(f32)
    embed = xb[1].astype(f32)
    trunk_scale = lax.rsqrt(pick(from_trunk, C) / D + EPS)
    embed_scale = lax.rsqrt(pick(from_embed, C) / D + EPS)
    mixed = trunk + trunk_scale * from_trunk[:, 0:C] + embed_scale * from_embed[:, 0:C]
    MX[zl] = mixed
    gains = gain[...]
    total = jnp.sum(mixed * mixed, axis=1, keepdims=True)
    high = total.astype(bf16).astype(f32)
    middle = (total - high).astype(bf16).astype(f32)
    low = total - high - middle
    pieces = jnp.where(lane == C, high, jnp.where(lane == C + 1, middle, low))
    Y8[z] = widen(mixed * gains, pieces).astype(bf16)
    y_s, y_r = slots(8), slots(8)
    for j in range(1, 8):
        send(lambda: Y8.at[z], lambda: Y8.at[z], y_s + j, y_r + z, dev(z_=add(z, j, 8)))
    m_s, m_r = slots(4), slots(4)
    for j in range(1, 4):
        send(
            lambda: MX.at[zl], lambda: MX.at[zl], m_s + j, m_r + zl, dev(z_=zh * 4 + add(zl, j, 4))
        )
    for j in range(1, 4):
        ht = add(h, j, 4)
        quarter = pl.ds(ht * 512, 512)
        pl.when(owner)(lambda: recv(UP.at[ozh, quarter], u_q + ht))
        send(
            lambda quarter=quarter: UP.at[ozh, quarter], lambda quarter=quarter: UP.at[ozh, quarter],
            u_b + j, u_q + ht, sib, owner,
        )
    for j in range(1, 8):
        zs = add(z, j, 8)
        recv(Y8.at[zs], y_r + zs)

    wide = Y8[...].astype(f32)
    ids = lax.broadcasted_iota(jnp.int32, wide.shape, 2)
    split = jnp.sum(
        jnp.where((ids >= C) & (ids < C + 3), wide, 0.0), axis=2, keepdims=True
    )
    part_squares = (split[0:4] + split[4:8]).reshape(N, 1)
    SB0[:, 0:N] = to_rows(part_squares)
    s0_s, s0_r = slots(8), slots(8)
    for j in range(1, 8):
        send(lambda: SB0, lambda: SY0.at[y], s0_s + j, s0_r + y, dev(y_=add(y, j, 8)))
    SY0[y] = SB0[...]

    @pl.when(owner)
    def _():
        own_u().wait()

    @pl.when(donor)
    def _():
        recv(UP.at[zh], u_f)
        for j in range(4):
            recv(UP.at[ozh, pl.ds(j * 512, 512)], u_q + j)

    y0 = Y8[0:4].reshape(N, CP)[:, 0:C]
    y1 = Y8[4:8].reshape(N, CP)[:, 0:C]

    def logits_block(at, carry):
        rows = pl.ds(pl.multiple_of(at * VC, VC), VC)
        LP[at] = dot(y0, UP[0, rows, :], 1, 1) + dot(y1, UP[1, rows, :], 1, 1)
        return carry

    lax.fori_loop(0, 8, logits_block, 0)
    l_s = slots(32)
    for i in range(8):
        for way in range(2):
            to = add(y, -1 - i, 8) if way == 0 else add(y, 1 + i, 8)
            for unit in range(2):
                rows = slice(way * 96 + unit * 48, way * 96 + unit * 48 + 48)
                idx = l_s + (way * 8 + i) * 2 + unit
                if i > 0:
                    recv(RL.at[to, rows], idx - 2)
                    LP[to, rows] = LP[to, rows] + RL[to, rows]
                if i < 7:
                    send(
                        lambda to=to, rows=rows: LP.at[to, rows],
                        lambda to=to, rows=rows: RL.at[to, rows],
                        idx, idx, right if way == 0 else left,
                    )
    for j in range(1, 8):
        ys = add(y, j, 8)
        recv(SY0.at[ys], s0_r + ys)
    all_squares = to_cols(jnp.sum(SY0[...], axis=0)[:, 0:N])
    mixed_scale = lax.rsqrt(pick(all_squares, 0) / D + EPS)
    MSC[...] = jnp.broadcast_to(mixed_scale, (N, 128)).reshape(4, R, 128)
    YN[0] = (y0.astype(f32) * mixed_scale).astype(bf16)
    YN[1] = (y1.astype(f32) * mixed_scale).astype(bf16)
    n_s = slots(1)
    send(lambda: YN.at[oc], lambda: YS, n_s, n_s, sib)

    logits = LP[y] * mixed_scale
    largest = jnp.max(logits, axis=1, keepdims=True)
    summed = jnp.sum(jnp.exp(logits - largest), axis=1, keepdims=True)
    SB1[:, 0:N] = to_rows(largest, summed)
    s1_s, s1_r = slots(8), slots(8)
    for j in range(1, 8):
        send(lambda: SB1, lambda: SY1.at[y], s1_s + j, s1_r + y, dev(y_=add(y, j, 8)))
    SY1[y] = SB1[...]

    def merge(ref):
        every = ref[...]
        top = jnp.max(every[:, 0:1, :], axis=0)
        whole = jnp.sum(every[:, 1:2, :] * jnp.exp(every[:, 0:1, :] - top[None]), axis=0)
        ids = lax.broadcasted_iota(jnp.int32, (8, VC), 0)
        return jnp.where(ids == 0, top, jnp.where(ids == 1, whole, 0.0))

    for j in range(1, 8):
        ys = add(y, j, 8)
        recv(SY1.at[ys], s1_r + ys)
    SB2[...] = merge(SY1)
    s2_s, s2_r = slots(8), slots(8)
    for j in range(1, 8):
        send(lambda: SB2, lambda: SZ2.at[z], s2_s + j, s2_r + z, dev(z_=add(z, j, 8)))
    SZ2[z] = SB2[...]
    for j in range(1, 8):
        zs = add(z, j, 8)
        recv(SZ2.at[zs], s2_r + zs)
    stats = to_cols(merge(SZ2)[:, 0:N])
    probs = jnp.exp(logits - pick(stats, 0)) / pick(stats, 1)
    vocab_ids = (zl * 4096 + zh * 2048 + y * VC) + lax.broadcasted_iota(jnp.int32, (N, VC), 1)
    hits = (vocab_ids == tgt[...]).astype(f32)
    GA[y] = (wt[...] * (probs - hits)).astype(bf16)

    g_s = slots(20)
    for i in range(5):
        for way in range(2):
            s = add(y, -i, 8) if way == 0 else add(y, i, 8)
            for half in range(2):
                rows = slice(half * 96, half * 96 + 96)
                idx = g_s + (way * 5 + i) * 2 + half
                if i > 0 and (i < 4 or half == way):
                    recv(GA.at[s, rows], idx - 2)
                if i < 3 or (i == 3 and half == way):
                    send(
                        lambda s=s, rows=rows: GA.at[s, rows], lambda s=s, rows=rows: GA.at[s, rows],
                        idx, idx, right if way == 0 else left,
                    )
    gs_s = slots(1)
    send(lambda: GA, lambda: GS, gs_s, gs_s, sib)

    GN[...] = jnp.zeros_like(GN)

    def normed_block(at, carry):
        rows = pl.ds(pl.multiple_of(at * VC, VC), VC)
        grads = GA[at]
        for zc in range(2):
            GN[zc] += dot(grads, UP[zc, rows, :], 1, 0)
        return carry

    lax.fori_loop(0, 8, normed_block, 0)
    NB[...] = GN[...].astype(bf16).reshape(8, R, C)
    n8_s, n8_r = slots(8), slots(8)
    for j in range(1, 8):
        zt = add(z, j, 8)
        send(lambda zt=zt: NB.at[zt], lambda: NR.at[z], n8_s + j, n8_r + z, dev(z_=zt))
    NR[z] = NB[z]

    recv(GS, gs_s)
    recv(YS, n_s)
    normed_mine = YN[c]
    normed_sib = YS[...]

    def vocab_block(at, carry):
        value = dot(GA[at], normed_mine, 0, 0) + dot(GS[at], normed_sib, 0, 0)
        VB[lax.div(at, 2), pl.ds(pl.multiple_of(lax.rem(at, 2) * VC, VC), VC), :] = value.astype(bf16)
        return carry

    lax.fori_loop(0, 8, vocab_block, 0)
    v_s, v_r = slots(4), slots(4)
    for j in range(1, 4):
        ht = add(h, j, 4)
        send(lambda ht=ht: VB.at[ht], lambda: VR.at[h], v_s + j, v_r + h, dev(h_=ht))
    VR[h] = VB[h]

    for j in range(1, 8):
        zs = add(z, j, 8)
        recv(NR.at[zs], n8_r + zs)
    for j in range(1, 4):
        zs = add(zl, j, 4)
        recv(MX.at[zs], m_r + zs)
    grad_normed = jnp.sum(NR[...].astype(f32), axis=0)
    scaled = grad_normed * gains
    inner = jnp.sum(scaled * (MX[zl] * MSC[zl][:, 0:1]), axis=1, keepdims=True)
    SG[zl] = widen(
        scaled, jnp.where(lane == C, inner, jnp.where(lane == C + 1, trunk_scale, embed_scale))
    )
    DCB[...] = jnp.broadcast_to(inner, (R, 128))
    d_s, d_r, e_s, e_r = slots(4), slots(4), slots(4), slots(4)
    for j in range(1, 4):
        zt = add(zl, j, 4)
        send(lambda: SG.at[zl], lambda: SG.at[zl], d_s + j, d_r + zl, dev(z_=zh * 4 + zt))
    for j in range(4):
        zt = add(zl, j, 4)
        send(lambda: DCB, lambda: DCR.at[zl], e_s + j, e_r + zl, dev(z_=ozh * 4 + zt))
    for j in range(1, 4):
        zs = add(zl, j, 4)
        recv(SG.at[zs], d_r + zs)
    for j in range(4):
        zs = add(zl, j, 4)
        recv(DCR.at[zs], e_r + zs)
    inner_part = (pick(SG[...], C) + pick(DCR[...], 0)).reshape(N, 1)
    SB3[:, 0:N] = to_rows(inner_part)
    s3_s, s3_r = slots(8), slots(8)
    for j in range(1, 8):
        send(lambda: SB3, lambda: SY3.at[y], s3_s + j, s3_r + y, dev(y_=add(y, j, 8)))
    SY3[y] = SB3[...]
    for j in range(1, 8):
        ys = add(y, j, 8)
        recv(SY3.at[ys], s3_r + ys)
    inner_all = pick(to_cols(jnp.sum(SY3[...], axis=0)[:, 0:N]), 0)
    mixed_normed = MX[...].reshape(N, C) * MSC[...].reshape(N, 128)[:, 0:1]
    scales = MSC[...].reshape(N, 128)[:, 0:1]
    grad_mixed = scales * (
        SG[...].reshape(N, CP)[:, 0:C] - mixed_normed * (inner_all / D)
    )
    GMF[...] = grad_mixed.reshape(4, R, C)
    grad_low = grad_mixed.astype(bf16)
    gathered = SG[...].reshape(N, CP)
    joined_scale = jnp.where(lax.div(zl, 2) == 0, pick(gathered, C + 1), pick(gathered, C + 2))
    grad_joined = (grad_mixed * joined_scale).astype(bf16)
    GML[...] = grad_joined
    c_s = slots(1)
    send(lambda: GML, lambda: GMS, c_s, c_s, sib)

    for q in range(8):
        value = dot(grad_low, W2[q // 4, (q % 4) * C : (q % 4 + 1) * C, :], 1, 1)
        JP[q // 2, (q % 2) * 4 : (q % 2) * 4 + 4] = value.astype(bf16).reshape(4, R, C)
    j_s = slots(16)
    for i in range(8):
        for way in range(2):
            to = add(y, -1 - i, 8) if way == 0 else add(y, 1 + i, 8)
            k = lax.rem(to, 4)
            cond = lax.div(to, 4) == hf
            for unit in range(2):
                part = pl.ds(way * 4 + unit * 2, 2)
                idx = j_s + (way * 4 + k) * 2 + unit

                def take():
                    recv(RJ.at[k, part], idx)
                    JP[k, part] = (JP[k, part].astype(f32) + RJ[k, part].astype(f32)).astype(bf16)

                if i > 0:
                    pl.when(cond)(take)
                if i < 7:
                    send(
                        lambda k=k, part=part: JP.at[k, part], lambda k=k, part=part: RJ.at[k, part],
                        idx, idx, right if way == 0 else left, cond,
                    )
    kind_mine = lax.div(zl, 2)
    k_s, k_r = slots(8), slots(4)
    for j in range(1, 8):
        zt = add(z, j, 8)
        send(
            lambda zt=zt: JP.at[ym, zt], lambda: SD.at[kind_mine, zh], k_s + j,
            k_r + kind_mine * 2 + zh, dev(z_=zt), in_half,
        )

    @pl.when(in_half)
    def _():
        SD[kind_mine, zh] = JP[ym, z]

    recv(GMS, c_s)
    recv(XS, x_s)
    grad_sib = GMS[...]
    for kk in range(2):
        for zz in range(2):
            q = kk * 2 + zz
            part = pl.ds(zz * 4, 4)
            cg[q * C : (q + 1) * C, :] = dot(
                XB[2 * c + kk, part].reshape(N, C), grad_joined, 0, 0
            ) + dot(XS[kk, part].reshape(N, C), grad_sib, 0, 0)

    for kind in range(2):
        for zs in range(2):
            z_from = zs * 4 + kind * 2 + yq
            pl.when(z_from != z)(lambda: recv(SD.at[kind, zs], k_r + kind * 2 + zs))
    trunk_side = SD[0, 0].astype(f32) + SD[0, 1].astype(f32)
    embed_side = SD[1, 0].astype(f32) + SD[1, 1].astype(f32)
    trunk_normed = trunk * trunk_scale
    embed_normed = embed * embed_scale
    PRE[...] = GMF[zl] + trunk_scale * trunk_side
    SB4[:, 0:R] = to_rows(
        jnp.sum(trunk_side * trunk_normed, axis=1, keepdims=True),
        jnp.sum(embed_side * embed_normed, axis=1, keepdims=True),
    )
    s4_s, s4_r = slots(8), slots(8)
    for j in range(1, 8):
        send(lambda: SB4, lambda: SY4.at[y], s4_s + j, s4_r + y, dev(y_=add(y, j, 8)))
    SY4[y] = SB4[...]
    o_s, o_r = slots(4), slots(4)
    for j in range(1, 4):
        send(lambda: PRE, lambda: XPR.at[h], o_s + j, o_r + h, dev(h_=add(h, j, 4)))
    XPR[h] = PRE[...]

    for j in range(1, 4):
        hs = add(h, j, 4)
        recv(VR.at[hs], v_r + hs)
    vocab_total = jnp.sum(VR[...].astype(f32), axis=0)
    ug[...] = vocab_total
    VSB[...] = vocab_total.astype(bf16)
    q_s = slots(1)
    send(lambda: VSB, lambda: VSR, q_s, q_s, dev(z_=ozh * 4 + zl, c_=oc), donor)

    for j in range(1, 8):
        ys = add(y, j, 8)
        recv(SY4.at[ys], s4_r + ys)
    SB5[...] = jnp.sum(SY4[...], axis=0)
    s5_s, s5_r = slots(8), slots(8)
    for j in range(4):
        for flip in range(2):
            if j + flip:
                send(
                    lambda: SB5, lambda: S7.at[h, zh], s5_s + j * 2 + flip, s5_r + h * 2 + zh,
                    dev(h_=add(h, j, 4), z_=(ozh if flip else zh) * 4 + zl),
                )
    S7[h, zh] = SB5[...]
    for j in range(4):
        for flip in range(2):
            if j + flip:
                hs, zs = add(h, j, 4), (ozh if flip else zh)
                recv(S7.at[hs, zs], s5_r + hs * 2 + zs)
    every = jnp.sum(S7[...], axis=(0, 1))
    same = S7[h, 0] + S7[h, 1]
    ids = lax.broadcasted_iota(jnp.int32, (8, 128), 0)
    dots = to_cols(jnp.where(ids == 0, every, same)[:, 0:R])
    eg[...] = embed_scale * (embed_side - embed_normed * (pick(dots, 1) / D))
    for j in range(1, 4):
        hs = add(h, j, 4)
        recv(XPR.at[hs], o_r + hs)
    tg[...] = jnp.sum(XPR[...], axis=0) - trunk_scale * trunk_normed * (pick(dots, 0) / D)

    @pl.when(donor)
    def _():
        recv(VSR, q_s)
        ug[...] = VSR[...].astype(f32)

    for cond, body in finals:
        when(cond, body)


def local(
    trunk_hidden, next_embeds, combine_weight, final_gain, unembed_weight, target_ids, loss_scale
):
    core = lax.rem(lax.axis_index("dp"), 2)
    both = jnp.stack([trunk_hidden, next_embeds[0]])

    def mine(values):
        return lax.dynamic_index_in_dim(
            values.reshape(4, 2, R), core, axis=1, keepdims=False
        ).reshape(N, 1)

    vm = lambda *shape: pltpu.VMEM(shape, f32)
    vb = lambda *shape: pltpu.VMEM(shape, bf16)
    scratch = [
        vb(2, 1280, C), vb(4, 8, R, C), vb(2, 8, R, C), vm(4, R, CP), vm(4, R, CP), vm(R, CP),
        vb(8, R, CP), vm(4, R, C), vb(2, V, C), vm(8, N, VC), vm(8, N, VC), vm(4, R, 128),
        vb(2, N, C), vb(N, C),
        vm(8, VC), vm(8, 8, VC), vm(8, VC), vm(8, 8, VC), vm(8, VC), vm(8, 8, VC),
        vb(8, N, VC), vb(8, N, VC), vm(2, N, C), vb(8, R, C), vb(8, R, C),
        vm(4, R, CP), vm(R, 128), vm(4, R, 128), vm(8, VC), vm(8, 8, VC),
        vm(4, R, C), vb(N, C), vb(N, C), vb(4, 8, R, C), vb(4, 8, R, C), vb(2, 2, R, C),
        vm(R, C), vm(4, R, C), vm(8, 128), vm(8, 8, 128), vm(8, 128), vm(4, 2, 8, 128),
        vb(4, 512, C), vb(4, 512, C), vb(512, C), vb(512, C),
        pltpu.SemaphoreType.DMA((320,)), pltpu.SemaphoreType.DMA((320,)), pltpu.SemaphoreType.DMA((2,)),
    ]
    spec = pl.BlockSpec(memory_space=pltpu.VMEM)
    trunk_grad, embed_grad, combine_grad, unembed_grad = pl.pallas_call(
        kernel,
        out_shape=(
            jax.ShapeDtypeStruct((R, C), f32),
            jax.ShapeDtypeStruct((R, C), f32),
            jax.ShapeDtypeStruct((1280, C), f32),
            jax.ShapeDtypeStruct((512, C), f32),
        ),
        in_specs=[spec] * 6,
        out_specs=(spec,) * 4,
        scratch_shapes=scratch,
        compiler_params=pltpu.CompilerParams(
            collective_id=0, has_side_effects=True, vmem_limit_bytes=60 * 1024 * 1024
        ),
    )(
        both,
        combine_weight[0],
        unembed_weight,
        final_gain.reshape(1, C),
        mine(target_ids[0]),
        mine(loss_scale[0]),
    )
    return trunk_grad, embed_grad[None], combine_grad[None], unembed_grad[None, None]


def solution(mesh):
    in_specs = (
        P("dp", "tensor"),
        P("head", "dp", "tensor"),
        P("head", "dp", "tensor"),
        P("tensor"),
        P("dp", "tensor"),
        P("head", None),
        P("head", None),
    )
    out_specs = (
        P("dp", "tensor"),
        P("head", "dp", "tensor"),
        P("head", "dp", "tensor"),
        P("dp", "head", None, "tensor"),
    )
    return jax.shard_map(local, mesh=mesh, in_specs=in_specs, out_specs=out_specs, check_vma=False)
```

```python
import jax
import jax.numpy as jnp
from jax import lax
from jax.experimental import pallas as pl
from jax.experimental.pallas import tpu as pltpu
from jax.sharding import PartitionSpec as P

D = 5120
EPS = 1e-05
R = 48
N = 192
C = 320
CP = 384
V = 2048
VC = 256
MESH = pl.DeviceIdType.MESH
HI = lax.Precision.HIGHEST
PAIRS = 128
SEMS = 256
f32 = jnp.float32
bf16 = jnp.bfloat16


def dot(left, right, a, b, precision=None):
    return lax.dot_general(
        left, right, (((a,), (b,)), ((), ())), precision=precision, preferred_element_type=f32
    )


def kernel(
    trunk_in, embed_in, w, u, gain, ids_in, scale_in,
    tg_out, eg_out, cg_out, ug_out,
    tg, eg, cg, ug,
    W2, XB, XS, PB, R2, T, Y8, MX, UP, LP, RL, MSC, YN, YS,
    SB0, SY0, SB1, SY1, SB2, SZ2, GA, GS, GN, NB, NR, SG, DCB, DCR, SB3, SY3, RL2, TW,
    GMF, GML, GMS, JP, RJ, SD, PRE, XPR, SB4, SY4, SB5, S7, VB, VR, VSB, VSR,
    ssem, rsem, lsem,
):
    h = lax.axis_index("head")
    t = lax.axis_index("tensor")
    d = lax.axis_index("dp")
    y, zh = lax.div(t, 2), lax.rem(t, 2)
    zl, c = lax.div(d, 2), lax.rem(d, 2)
    z = zh * 4 + zl
    oc, ozh = 1 - c, 1 - zh

    def dev(h_=None, y_=None, z_=None, c_=None):
        h_ = h if h_ is None else h_
        y_ = y if y_ is None else y_
        z_ = z if z_ is None else z_
        c_ = c if c_ is None else c_
        return (h_, y_ * 2 + lax.div(z_, 4), lax.rem(z_, 4) * 2 + c_)

    def add(value, step, size):
        return lax.rem(value + (step + size), size)

    sib = dev(c_=oc)
    right, left = dev(y_=add(y, 1, 8)), dev(y_=add(y, -1, 8))
    me = dev()

    counts = {"both": 0, "s": PAIRS, "r": PAIRS}

    def slots(n, which="both"):
        first = counts[which]
        counts[which] += n
        return first

    def some(sends, receives):
        return slots(sends, "s"), slots(receives, "r")

    finals = []

    def copy(src, dst, s, r, to):
        return pltpu.make_async_remote_copy(
            src_ref=src, dst_ref=dst, send_sem=ssem.at[s], recv_sem=rsem.at[r],
            device_id=to, device_id_type=MESH,
        )

    def when(cond, body):
        if cond is None:
            body()
        else:
            pl.when(cond)(body)

    def send(src, dst, s, r, to, cond=None):
        when(cond, lambda: copy(src(), dst(), s, r, to).start())
        finals.append((cond, lambda: copy(src(), dst(), s, r, to).wait_send()))

    def recv(dst, r):
        copy(dst, dst, 0, r, me).wait_recv()

    def put(at):
        pairs = ((tg, tg_out), (eg, eg_out), (cg, cg_out), (ug, ug_out))
        return pltpu.make_async_copy(*pairs[at], lsem.at[2 + at])

    lane = lax.broadcasted_iota(jnp.int32, (R, CP), 1)
    e8 = (
        lax.broadcasted_iota(jnp.int32, (8, 128), 0) == lax.broadcasted_iota(jnp.int32, (8, 128), 1)
    ).astype(f32)

    def pick(x, at):
        ids = lax.broadcasted_iota(jnp.int32, x.shape, x.ndim - 1)
        return jnp.sum(jnp.where(ids == at, x, 0.0), axis=-1, keepdims=True)

    def to_rows(first, second=None):
        ids = lax.broadcasted_iota(jnp.int32, (first.shape[0], 128), 1)
        v = jnp.where(ids == 0, first, 0.0)
        if second is not None:
            v = jnp.where(ids == 1, second, v)
        return dot(e8, v, 1, 1, HI)

    def to_cols(rows):
        return dot(rows, e8, 0, 0, HI)

    def widen(value, extra):
        T[:, 0:C] = value
        return jnp.where(lane >= C, extra, T[...])

    barrier = pltpu.get_barrier_semaphore()
    peers = [dev(y_=add(y, j, 8)) for j in range(1, 8)]
    peers += [dev(z_=add(z, j, 8)) for j in range(1, 8)]
    peers += [dev(h_=add(h, j, 4)) for j in range(1, 4)]
    peers += [dev(h_=add(h, j, 4), z_=ozh * 4 + zl) for j in range(1, 4)]
    peers += [sib, dev(z_=ozh * 4 + zl, c_=oc)]
    for to in peers:
        pl.semaphore_signal(barrier, inc=1, device_id=to, device_id_type=MESH)
    own_w = pltpu.make_async_copy(w, W2.at[c], lsem.at[0])
    own_w.start()
    T[...] = jnp.zeros_like(T)
    for ref in (SB0, SB1, SB2, SB3, SB4, SB5, DCB):
        ref[...] = jnp.zeros_like(ref)
    PB[...] = jnp.zeros_like(PB)
    two = lax.broadcasted_iota(jnp.int32, (8, 384), 0)
    TW[...] = to_cols(
        jnp.where(two == 0, ids_in[...].astype(f32), jnp.where(two == 1, scale_in[...], 0.0))
    ).reshape(4, 2, R, 128)
    chosen = jnp.concatenate([TW[j, c] for j in range(4)], axis=0)
    targets, weights = pick(chosen, 0), pick(chosen, 1)
    pl.semaphore_wait(barrier, len(peers))

    yq, ym = lax.div(y, 4), lax.rem(y, 4)
    hf = lax.rem(zl, 2)
    in_half = hf == yq
    a_s, a_r = some(4, 8)
    for kind in range(2):
        for zh_to in range(2):
            z_to = zh_to * 4 + kind * 2 + yq
            send(
                lambda kind=kind: (trunk_in, embed_in)[kind], lambda: XB.at[ym, z],
                a_s + kind * 2 + zh_to, a_r + z, dev(z_=z_to), z_to != z,
            )

            def keep(kind=kind):
                XB[ym, z] = (trunk_in, embed_in)[kind][...]

            pl.when(z_to == z)(keep)
    w_s = slots(1)
    send(lambda: w, lambda: W2.at[c], w_s, w_s, sib)

    owner = c == zh
    donor = c != zh
    u_f = slots(1)
    u_x, u_q = some(9, 4)
    u_b, u_d = u_x + 4, u_x + 8
    own_u = lambda: pltpu.make_async_copy(u, UP.at[zh], lsem.at[1])
    pl.when(owner)(lambda: own_u().start())

    def quarter_of(at):
        return pl.ds(pl.multiple_of(at * 512, 512), 512)

    mine = quarter_of(h)
    b_s = slots(32)
    for i in range(8):
        for unit in range(4):
            for way in range(2):
                s = add(y, -i, 8) if way == 0 else add(y, i, 8)
                k = lax.rem(s, 4)
                cond = lax.div(s, 4) == hf
                zs = way * 4 + unit
                idx = b_s + k * 8 + zs
                if i == 0:
                    pl.when(in_half & (z != zs))(lambda: recv(XB.at[ym, zs], a_r + zs))
                else:
                    pl.when(cond)(lambda: recv(XB.at[k, zs], idx))
                if i < 7:
                    send(
                        lambda k=k, zs=zs: XB.at[k, zs], lambda k=k, zs=zs: XB.at[k, zs],
                        idx, idx, right if way == 0 else left, cond,
                    )
        if i == 1:
            send(
                lambda: u.at[:, mine], lambda: UP.at[zh, :, mine], u_d, u_q + h,
                dev(z_=ozh * 4 + zl), donor,
            )

    send(lambda: u, lambda: UP.at[zh], u_f, u_f, sib, owner)
    pl.when(owner)(lambda: recv(UP.at[ozh, :, mine], u_q + h))
    for j in range(1, 4):
        send(
            lambda: UP.at[ozh, :, mine], lambda: UP.at[ozh, :, mine], u_x + j, u_q + h,
            dev(h_=add(h, j, 4)), owner,
        )
    send(lambda: UP.at[ozh, :, mine], lambda: UP.at[ozh, :, mine], u_b, u_q + h, sib, owner)

    own_w.wait()
    recv(W2.at[oc], w_s)
    acc = jnp.zeros((N, C), f32)
    squares = jnp.zeros((N, 1), f32)
    for q in range(8):
        block = XB[q // 2, (q % 2) * 4 : (q % 2) * 4 + 4].reshape(N, C)
        acc = acc + dot(block, W2[q // 4, :, (q % 4) * C : (q % 4 + 1) * C], 1, 1)
        wide = block.astype(f32)
        squares = squares + jnp.sum(wide * wide, axis=1, keepdims=True)
    PB[:, :, 0:C] = acc.reshape(4, R, C)
    lane3 = lax.broadcasted_iota(jnp.int32, (4, R, CP), 2)
    PB[...] = jnp.where(lane3 >= C, squares.reshape(4, R, 1), PB[...])
    p_s, p_r = some(4, 4)
    for j in range(1, 4):
        zt = add(zl, j, 4)
        send(
            lambda zt=zt: PB.at[zt], lambda: R2.at[zl], p_s + j, p_r + zl, dev(z_=zh * 4 + zt)
        )
    R2[zl] = PB[zl]
    x_s = slots(1)
    send(lambda: XB.at[pl.ds(2 * oc, 2)], lambda: XS, x_s, x_s, sib)
    for j in range(1, 4):
        zt = add(zl, j, 4)
        recv(R2.at[zt], p_r + zt)
    from_trunk = R2[0] + R2[1]
    from_embed = R2[2] + R2[3]
    trunk = trunk_in[...].astype(f32)
    embed = embed_in[...].astype(f32)
    trunk_scale = lax.rsqrt(pick(from_trunk, C) / D + EPS)
    embed_scale = lax.rsqrt(pick(from_embed, C) / D + EPS)
    mixed = trunk + trunk_scale * from_trunk[:, 0:C] + embed_scale * from_embed[:, 0:C]
    MX[zl] = mixed
    gains = gain[...].reshape(1, C)
    total = jnp.sum(mixed * mixed, axis=1, keepdims=True)
    high = total.astype(bf16).astype(f32)
    middle = (total - high).astype(bf16).astype(f32)
    low = total - high - middle
    pieces = jnp.where(lane == C, high, jnp.where(lane == C + 1, middle, low))
    Y8[z] = widen(mixed * gains, pieces).astype(bf16)
    y_s, y_r = some(8, 8)
    for j in range(1, 8):
        send(lambda: Y8.at[z], lambda: Y8.at[z], y_s + j, y_r + z, dev(z_=add(z, j, 8)))
    for j in range(1, 4):
        ht = add(h, j, 4)
        quarter = quarter_of(ht)
        pl.when(owner)(lambda: recv(UP.at[ozh, :, quarter], u_q + ht))
        send(
            lambda quarter=quarter: UP.at[ozh, :, quarter], lambda quarter=quarter: UP.at[ozh, :, quarter],
            u_b + j, u_q + ht, sib, owner,
        )
    for j in range(1, 8):
        zs = add(z, j, 8)
        recv(Y8.at[zs], y_r + zs)
    m_s, m_r = some(4, 4)
    for j in range(1, 4):
        send(
            lambda: MX.at[zl], lambda: MX.at[zl], m_s + j, m_r + zl, dev(z_=zh * 4 + add(zl, j, 4))
        )

    wide = Y8[...].astype(f32)
    ids = lax.broadcasted_iota(jnp.int32, wide.shape, 2)
    split = jnp.sum(
        jnp.where((ids >= C) & (ids < C + 3), wide, 0.0), axis=2, keepdims=True
    )
    part_squares = (split[0:4] + split[4:8]).reshape(N, 1)
    SB0[:, 0:N] = to_rows(part_squares)
    s0_s, s0_r = some(8, 8)
    for j in range(1, 8):
        send(lambda: SB0, lambda: SY0.at[y], s0_s + j, s0_r + y, dev(y_=add(y, j, 8)))
    SY0[y] = SB0[...]

    @pl.when(owner)
    def _():
        own_u().wait()

    @pl.when(donor)
    def _():
        recv(UP.at[zh], u_f)
        for j in range(4):
            recv(UP.at[ozh, :, pl.ds(j * 512, 512)], u_q + j)

    y0 = Y8[0:4].reshape(N, CP)[:, 0:C]
    y1 = Y8[4:8].reshape(N, CP)[:, 0:C]

    def logits_block(at):
        cols = pl.ds(pl.multiple_of(at * VC, VC), VC)
        LP[at] = dot(y0, UP[0, :, cols], 1, 0) + dot(y1, UP[1, :, cols], 1, 0)

    l_s = slots(32)

    def hop(o, way, unit, got):
        to = add(y, o, 8) if way == 0 else add(y, -o, 8)
        rows = slice(unit * R, unit * R + R)
        idx = l_s + (way * 4 + o) * 4 + unit
        if got:
            last = RL2 if (o == 0 and way == 1) else RL.at[to]
            recv(last.at[rows], idx)
            LP[to, rows] = LP[to, rows] + last[rows]
        if o:
            place = RL2 if (o == 1 and way == 1) else RL.at[to]
            send(
                lambda: LP.at[to, rows], lambda: place.at[rows], idx - 4, idx - 4,
                right if way == 0 else left,
            )

    logits_block(add(y, 4, 8))
    for unit in range(2):
        hop(4, 0, unit, False)
        hop(4, 1, unit + 2, False)
    logits_block(add(y, 3, 8))
    logits_block(add(y, -3, 8))
    for unit in range(2):
        hop(3, 0, unit + 2, False)
        hop(3, 1, unit, False)
    logits_block(add(y, 2, 8))
    logits_block(add(y, -2, 8))
    for unit in range(2):
        hop(3, 0, unit, True)
        hop(3, 1, unit + 2, True)
    logits_block(add(y, 1, 8))
    logits_block(add(y, -1, 8))
    logits_block(y)
    for o in (2, 1, 0):
        for unit in (2, 3, 0, 1):
            hop(o, 0, unit, True)
            hop(o, 1, (unit + 2) % 4, True)
    for j in range(1, 8):
        ys = add(y, j, 8)
        recv(SY0.at[ys], s0_r + ys)
    all_squares = to_cols(jnp.sum(SY0[...], axis=0)[:, 0:N])
    mixed_scale = lax.rsqrt(pick(all_squares, 0) / D + EPS)
    MSC[...] = jnp.broadcast_to(mixed_scale, (N, 128)).reshape(4, R, 128)
    YN[0] = (y0.astype(f32) * mixed_scale).astype(bf16)
    YN[1] = (y1.astype(f32) * mixed_scale).astype(bf16)
    n_s = slots(1)
    send(lambda: YN.at[oc], lambda: YS, n_s, n_s, sib)

    logits = LP[y] * mixed_scale
    largest = jnp.max(logits, axis=1, keepdims=True)
    summed = jnp.sum(jnp.exp(logits - largest), axis=1, keepdims=True)
    SB1[:, 0:N] = to_rows(largest, summed)
    s1_s, s1_r = some(8, 8)
    for j in range(1, 8):
        send(lambda: SB1, lambda: SY1.at[y], s1_s + j, s1_r + y, dev(y_=add(y, j, 8)))
    SY1[y] = SB1[...]

    def merge(ref):
        every = ref[...]
        top = jnp.max(every[:, 0:1, :], axis=0)
        whole = jnp.sum(every[:, 1:2, :] * jnp.exp(every[:, 0:1, :] - top[None]), axis=0)
        ids = lax.broadcasted_iota(jnp.int32, (8, VC), 0)
        return jnp.where(ids == 0, top, jnp.where(ids == 1, whole, 0.0))

    for j in range(1, 8):
        ys = add(y, j, 8)
        recv(SY1.at[ys], s1_r + ys)
    SB2[...] = merge(SY1)
    s2_s, s2_r = some(8, 8)
    for j in range(1, 8):
        send(lambda: SB2, lambda: SZ2.at[z], s2_s + j, s2_r + z, dev(z_=add(z, j, 8)))
    SZ2[z] = SB2[...]
    for j in range(1, 8):
        zs = add(z, j, 8)
        recv(SZ2.at[zs], s2_r + zs)
    stats = to_cols(merge(SZ2)[:, 0:N])
    probs = jnp.exp(logits - pick(stats, 0)) / pick(stats, 1)
    vocab_ids = (zl * 4096 + zh * 2048 + y * VC) + lax.broadcasted_iota(jnp.int32, (N, VC), 1)
    hits = (vocab_ids.astype(f32) == targets).astype(f32)
    GA[y] = (weights * (probs - hits)).astype(bf16)

    g_s = slots(20)
    for i in range(5):
        for way in range(2):
            s = add(y, -i, 8) if way == 0 else add(y, i, 8)
            for half in range(2):
                rows = slice(half * 96, half * 96 + 96)
                idx = g_s + (way * 5 + i) * 2 + half
                if i > 0 and (i < 4 or half == way):
                    recv(GA.at[s, rows], idx - 2)
                if i < 3 or (i == 3 and half == way):
                    send(
                        lambda s=s, rows=rows: GA.at[s, rows], lambda s=s, rows=rows: GA.at[s, rows],
                        idx, idx, right if way == 0 else left,
                    )
    gs_s = slots(1)
    send(lambda: GA, lambda: GS, gs_s, gs_s, sib)

    GN[...] = jnp.zeros_like(GN)

    def normed_block(at, carry):
        rows = pl.ds(pl.multiple_of(at * VC, VC), VC)
        grads = GA[at]
        for zc in range(2):
            GN[zc] += dot(grads, UP[zc, :, rows], 1, 1)
        return carry

    lax.fori_loop(0, 8, normed_block, 0)
    NB[...] = GN[...].astype(bf16).reshape(8, R, C)
    n8_s, n8_r = some(8, 8)
    for j in range(1, 8):
        zt = add(z, j, 8)
        send(lambda zt=zt: NB.at[zt], lambda: NR.at[z], n8_s + j, n8_r + z, dev(z_=zt))
    NR[z] = NB[z]

    for j in range(1, 8):
        zs = add(z, j, 8)
        recv(NR.at[zs], n8_r + zs)
    for j in range(1, 4):
        zs = add(zl, j, 4)
        recv(MX.at[zs], m_r + zs)
    grad_normed = jnp.sum(NR[...].astype(f32), axis=0)
    scaled = grad_normed * gains
    inner = jnp.sum(scaled * (MX[zl] * MSC[zl][:, 0:1]), axis=1, keepdims=True)
    SG[zl] = widen(
        scaled, jnp.where(lane == C, inner, jnp.where(lane == C + 1, trunk_scale, embed_scale))
    )
    DCB[:, 0:R] = to_rows(inner)
    d_s, d_r = some(4, 4)
    e_s, e_r = some(4, 4)
    for j in range(1, 4):
        zt = add(zl, j, 4)
        send(lambda: SG.at[zl], lambda: SG.at[zl], d_s + j, d_r + zl, dev(z_=zh * 4 + zt))
    for j in range(4):
        zt = add(zl, j, 4)
        send(lambda: DCB, lambda: DCR.at[zl], e_s + j, e_r + zl, dev(z_=ozh * 4 + zt))
    recv(GS, gs_s)
    recv(YS, n_s)
    normed_mine = YN[c]
    normed_sib = YS[...]

    def vocab_block(at, carry):
        value = dot(normed_mine, GA[at], 0, 0) + dot(normed_sib, GS[at], 0, 0)
        VB[lax.div(at, 2), :, pl.ds(pl.multiple_of(lax.rem(at, 2) * VC, VC), VC)] = value.astype(bf16)
        return carry

    lax.fori_loop(0, 8, vocab_block, 0)
    v_s, v_r = some(4, 4)
    for j in range(1, 4):
        ht = add(h, j, 4)
        send(lambda ht=ht: VB.at[ht], lambda: VR.at[h], v_s + j, v_r + h, dev(h_=ht))
    VR[h] = VB[h]

    for j in range(1, 4):
        zs = add(zl, j, 4)
        recv(SG.at[zs], d_r + zs)
    for j in range(4):
        zs = add(zl, j, 4)
        recv(DCR.at[zs], e_r + zs)
    other = jnp.concatenate([to_cols(DCR[j][:, 0:R]) for j in range(4)], axis=0)
    inner_part = pick(SG[...], C).reshape(N, 1) + pick(other, 0)
    SB3[:, 0:N] = to_rows(inner_part)
    s3_s, s3_r = some(8, 8)
    for j in range(1, 8):
        send(lambda: SB3, lambda: SY3.at[y], s3_s + j, s3_r + y, dev(y_=add(y, j, 8)))
    SY3[y] = SB3[...]
    for j in range(1, 8):
        ys = add(y, j, 8)
        recv(SY3.at[ys], s3_r + ys)
    inner_all = pick(to_cols(jnp.sum(SY3[...], axis=0)[:, 0:N]), 0)
    mixed_normed = MX[...].reshape(N, C) * MSC[...].reshape(N, 128)[:, 0:1]
    scales = MSC[...].reshape(N, 128)[:, 0:1]
    grad_mixed = scales * (
        SG[...].reshape(N, CP)[:, 0:C] - mixed_normed * (inner_all / D)
    )
    GMF[...] = grad_mixed.reshape(4, R, C)
    grad_low = grad_mixed.astype(bf16)
    gathered = SG[...].reshape(N, CP)
    joined_scale = jnp.where(lax.div(zl, 2) == 0, pick(gathered, C + 1), pick(gathered, C + 2))
    grad_joined = (grad_mixed * joined_scale).astype(bf16)
    GML[...] = grad_joined
    c_s = slots(1)
    send(lambda: GML, lambda: GMS, c_s, c_s, sib)

    for q in range(8):
        value = dot(grad_low, W2[q // 4, :, (q % 4) * C : (q % 4 + 1) * C], 1, 0)
        JP[q // 2, (q % 2) * 4 : (q % 2) * 4 + 4] = value.astype(bf16).reshape(4, R, C)
    q_s = slots(1)

    def sum_vocab():
        for j in range(1, 4):
            hs = add(h, j, 4)
            recv(VR.at[hs], v_r + hs)
        vocab_total = jnp.sum(VR[...].astype(f32), axis=0)
        ug[...] = vocab_total
        VSB[...] = vocab_total.astype(bf16)
        send(lambda: VSB, lambda: VSR, q_s, q_s, dev(z_=ozh * 4 + zl, c_=oc), donor)

    j_s = slots(32)
    for i in range(8):
        for unit in range(4):
            for way in range(2):
                to = add(y, -1 - i, 8) if way == 0 else add(y, 1 + i, 8)
                k = lax.rem(to, 4)
                cond = lax.div(to, 4) == hf
                part = way * 4 + unit
                idx = j_s + k * 8 + part

                def take():
                    recv(RJ.at[k, part], idx)
                    JP[k, part] = (JP[k, part].astype(f32) + RJ[k, part].astype(f32)).astype(bf16)

                if i > 0:
                    pl.when(cond)(take)
                if i < 7:
                    send(
                        lambda k=k, part=part: JP.at[k, part], lambda k=k, part=part: RJ.at[k, part],
                        idx, idx, right if way == 0 else left, cond,
                    )
        if i == 0:
            sum_vocab()
    kind_mine = lax.div(zl, 2)
    k_s, k_r = some(8, 4)
    for j in range(1, 8):
        zt = add(z, j, 8)
        send(
            lambda zt=zt: JP.at[ym, zt], lambda: SD.at[kind_mine, zh], k_s + j,
            k_r + kind_mine * 2 + zh, dev(z_=zt), in_half,
        )

    @pl.when(in_half)
    def _():
        SD[kind_mine, zh] = JP[ym, z]

    recv(GMS, c_s)
    recv(XS, x_s)
    grad_sib = GMS[...]
    for kk in range(2):
        for zz in range(2):
            q = kk * 2 + zz
            part = pl.ds(zz * 4, 4)
            cg[:, q * C : (q + 1) * C] = dot(
                grad_joined, XB[2 * c + kk, part].reshape(N, C), 0, 0
            ) + dot(grad_sib, XS[kk, part].reshape(N, C), 0, 0)

    put(2).start()
    for kind in range(2):
        for zs in range(2):
            z_from = zs * 4 + kind * 2 + yq
            pl.when(z_from != z)(lambda: recv(SD.at[kind, zs], k_r + kind * 2 + zs))
    trunk_side = SD[0, 0].astype(f32) + SD[0, 1].astype(f32)
    embed_side = SD[1, 0].astype(f32) + SD[1, 1].astype(f32)
    trunk_normed = trunk * trunk_scale
    embed_normed = embed * embed_scale
    PRE[...] = GMF[zl] + trunk_scale * trunk_side
    SB4[:, 0:R] = to_rows(
        jnp.sum(trunk_side * trunk_normed, axis=1, keepdims=True),
        jnp.sum(embed_side * embed_normed, axis=1, keepdims=True),
    )
    s4_s, s4_r = some(8, 8)
    for j in range(1, 8):
        send(lambda: SB4, lambda: SY4.at[y], s4_s + j, s4_r + y, dev(y_=add(y, j, 8)))
    SY4[y] = SB4[...]
    o_s, o_r = some(4, 4)
    for j in range(1, 4):
        send(lambda: PRE, lambda: XPR.at[h], o_s + j, o_r + h, dev(h_=add(h, j, 4)))
    XPR[h] = PRE[...]

    for j in range(1, 8):
        ys = add(y, j, 8)
        recv(SY4.at[ys], s4_r + ys)
    SB5[...] = jnp.sum(SY4[...], axis=0)
    s5_s, s5_r = some(8, 8)
    for j in range(4):
        for flip in range(2):
            if j + flip:
                send(
                    lambda: SB5, lambda: S7.at[h, zh], s5_s + j * 2 + flip, s5_r + h * 2 + zh,
                    dev(h_=add(h, j, 4), z_=(ozh if flip else zh) * 4 + zl),
                )
    S7[h, zh] = SB5[...]
    for j in range(4):
        for flip in range(2):
            if j + flip:
                hs, zs = add(h, j, 4), (ozh if flip else zh)
                recv(S7.at[hs, zs], s5_r + hs * 2 + zs)
    every = jnp.sum(S7[...], axis=(0, 1))
    same = S7[h, 0] + S7[h, 1]
    ids = lax.broadcasted_iota(jnp.int32, (8, 128), 0)
    dots = to_cols(jnp.where(ids == 0, every, same)[:, 0:R])
    pl.when(owner)(lambda: put(3).start())
    eg[...] = embed_scale * (embed_side - embed_normed * (pick(dots, 1) / D))
    put(1).start()
    for j in range(1, 4):
        hs = add(h, j, 4)
        recv(XPR.at[hs], o_r + hs)
    tg[...] = jnp.sum(XPR[...], axis=0) - trunk_scale * trunk_normed * (pick(dots, 0) / D)

    put(0).start()

    @pl.when(donor)
    def _():
        recv(VSR, q_s)
        ug[...] = VSR[...].astype(f32)
        put(3).start()

    for at in range(4):
        put(at).wait()
    assert counts["both"] <= PAIRS and max(counts.values()) <= SEMS
    for cond, body in finals:
        when(cond, body)


def put_out(*refs):
    into, out, held, sems = refs[:4], refs[4:8], refs[8:12], refs[12]
    reads = [pltpu.make_async_copy(into[k], held[k], sems.at[k]) for k in range(4)]
    writes = [pltpu.make_async_copy(held[k], out[k], sems.at[k + 4]) for k in range(4)]
    order = (2, 3, 0, 1)
    for k in order:
        reads[k].start()
    for k in order:
        reads[k].wait()
        writes[k].start()
    for k in order:
        writes[k].wait()


def local(
    trunk_hidden, next_embeds, combine_weight, final_gain, unembed_weight, target_ids, loss_scale
):
    vm = lambda *shape: pltpu.VMEM(shape, f32)
    vb = lambda *shape: pltpu.VMEM(shape, bf16)
    scratch = [
        vm(R, C), vm(R, C), vm(C, 1280), vm(C, 512),
        vb(2, C, 1280), vb(4, 8, R, C), vb(2, 8, R, C), vm(4, R, CP), vm(4, R, CP), vm(R, CP),
        vb(8, R, CP), vm(4, R, C), vb(2, C, V), vm(8, N, VC), vm(8, N, VC), vm(4, R, 128),
        vb(2, N, C), vb(N, C),
        vm(8, VC), vm(8, 8, VC), vm(8, VC), vm(8, 8, VC), vm(8, VC), vm(8, 8, VC),
        vb(8, N, VC), vb(8, N, VC), vm(2, N, C), vb(8, R, C), vb(8, R, C),
        vm(4, R, CP), vm(8, 128), vm(4, 8, 128), vm(8, VC), vm(8, 8, VC),
        vm(N, VC), vm(4, 2, R, 128),
        vm(4, R, C), vb(N, C), vb(N, C), vb(4, 8, R, C), vb(4, 8, R, C), vb(2, 2, R, C),
        vm(R, C), vm(4, R, C), vm(8, 128), vm(8, 8, 128), vm(8, 128), vm(4, 2, 8, 128),
        vb(4, C, 512), vb(4, C, 512), vb(C, 512), vb(C, 512),
        pltpu.SemaphoreType.DMA((SEMS,)), pltpu.SemaphoreType.DMA((SEMS,)), pltpu.SemaphoreType.DMA((6,)),
    ]
    spec = pl.BlockSpec(memory_space=pltpu.VMEM)
    remote = pl.BlockSpec(memory_space=pl.ANY)
    trunk_grad, embed_grad, combine_grad, unembed_grad = pl.pallas_call(
        kernel,
        out_shape=(
            jax.ShapeDtypeStruct((R, C), f32),
            jax.ShapeDtypeStruct((R, C), f32),
            jax.ShapeDtypeStruct((C, 1280), f32),
            jax.ShapeDtypeStruct((C, 512), f32),
        ),
        in_specs=[spec, spec, remote, remote, spec, spec, spec],
        out_specs=(remote,) * 4,
        scratch_shapes=scratch,
        compiler_params=pltpu.CompilerParams(
            collective_id=0, has_side_effects=True, vmem_limit_bytes=60 * 1024 * 1024
        ),
    )(
        trunk_hidden,
        next_embeds[0],
        combine_weight[0].T,
        unembed_weight.T,
        final_gain,
        target_ids,
        loss_scale,
    )
    results = (trunk_grad, embed_grad, combine_grad, unembed_grad)
    trunk_grad, embed_grad, combine_grad, unembed_grad = pl.pallas_call(
        put_out,
        out_shape=tuple(jax.ShapeDtypeStruct(r.shape, r.dtype) for r in results),
        in_specs=[remote] * 4,
        out_specs=(remote,) * 4,
        scratch_shapes=[pltpu.VMEM(r.shape, r.dtype) for r in results]
        + [pltpu.SemaphoreType.DMA((8,))],
        compiler_params=pltpu.CompilerParams(vmem_limit_bytes=60 * 1024 * 1024),
    )(*results)
    return trunk_grad, embed_grad[None], combine_grad.T[None], unembed_grad.T[None, None]


def solution(mesh):
    in_specs = (
        P("dp", "tensor"),
        P("head", "dp", "tensor"),
        P("head", "dp", "tensor"),
        P("tensor"),
        P("dp", "tensor"),
        P("head", None),
        P("head", None),
    )
    out_specs = (
        P("dp", "tensor"),
        P("head", "dp", "tensor"),
        P("head", "dp", "tensor"),
        P("dp", "head", None, "tensor"),
    )
    return jax.shard_map(local, mesh=mesh, in_specs=in_specs, out_specs=out_specs, check_vma=False)
```

```python
import jax
import jax.numpy as jnp
from jax import lax
from jax.experimental import pallas as pl
from jax.experimental.pallas import tpu as pltpu
from jax.sharding import PartitionSpec as P

D = 5120
EPS = 1e-05
R = 48
N = 192
C = 320
CP = 384
V = 2048
VC = 256
MESH = pl.DeviceIdType.MESH
HI = lax.Precision.HIGHEST
POOL = 64
SEMS = 239
f32 = jnp.float32
bf16 = jnp.bfloat16


def dot(left, right, a, b, precision=None):
    return lax.dot_general(
        left, right, (((a,), (b,)), ((), ())), precision=precision, preferred_element_type=f32
    )


def kernel(
    trunk_in, embed_in, w, u, gain, ids_in, scale_in,
    tg_out, eg_out, cg_out, ug_out,
    tg, eg, cg, ug,
    W2, XB, XS, PF, PB, R2, T, Y8, MX, UP, LP, RL, MSC, YN, YS,
    SB0, SY0, SB1, SY1, SB2, SZ2, GA, GS, GN, NB, NR, INN, SB3, SY3, SB6, SZ6, RL2, TW,
    GMF, GMB, GML, GMS, JP, RJ, RJ2, SD, PRE, XPR, SB4, SY4, SB5, SZ5, SB7, S7, VB, VR, VSB, VSR,
    ssem, rsem, lsem,
):
    h = lax.axis_index("head")
    t = lax.axis_index("tensor")
    d = lax.axis_index("dp")
    y, zh = lax.div(t, 2), lax.rem(t, 2)
    zl, c = lax.div(d, 2), lax.rem(d, 2)
    z = zh * 4 + zl
    oc, ozh = 1 - c, 1 - zh

    def dev(h_=None, y_=None, z_=None, c_=None):
        h_ = h if h_ is None else h_
        y_ = y if y_ is None else y_
        z_ = z if z_ is None else z_
        c_ = c if c_ is None else c_
        return (h_, y_ * 2 + lax.div(z_, 4), lax.rem(z_, 4) * 2 + c_)

    def add(value, step, size):
        return lax.rem(value + (step + size), size)

    sib = dev(c_=oc)
    right, left = dev(y_=add(y, 1, 8)), dev(y_=add(y, -1, 8))
    me = dev()

    counts = {"r": 0}

    def slots(n):
        first = counts["r"]
        counts["r"] += n
        return first

    def some(sends, receives):
        return 0, slots(receives)

    finals = []

    def copy(src, dst, s, r, to):
        return pltpu.make_async_remote_copy(
            src_ref=src, dst_ref=dst, send_sem=ssem.at[s], recv_sem=rsem.at[r],
            device_id=to, device_id_type=MESH,
        )

    def when(cond, body):
        if cond is None:
            body()
        else:
            pl.when(cond)(body)

    def send(src, dst, s, r, to, cond=None):
        at = len(finals) % POOL
        if len(finals) >= POOL:
            when(*finals[-POOL])
        when(cond, lambda: copy(src(), dst(), at, r, to).start())
        finals.append((cond, lambda: copy(src(), dst(), at, r, to).wait_send()))

    def recv(dst, r):
        copy(dst, dst, 0, r, me).wait_recv()

    def put(at):
        pairs = ((tg, tg_out), (eg, eg_out), (cg, cg_out), (ug, ug_out))
        return pltpu.make_async_copy(*pairs[at], lsem.at[2 + at])

    lane = lax.broadcasted_iota(jnp.int32, (R, CP), 1)
    e8 = (
        lax.broadcasted_iota(jnp.int32, (8, 128), 0) == lax.broadcasted_iota(jnp.int32, (8, 128), 1)
    ).astype(f32)

    def pick(x, at):
        ids = lax.broadcasted_iota(jnp.int32, x.shape, x.ndim - 1)
        return jnp.sum(jnp.where(ids == at, x, 0.0), axis=-1, keepdims=True)

    def picks(x, at, n):
        ids = lax.broadcasted_iota(jnp.int32, x.shape, x.ndim - 1)
        return jnp.sum(jnp.where((ids >= at) & (ids < at + n), x, 0.0), axis=-1, keepdims=True)

    def in_three(total, at, ids, rest):
        high = total.astype(bf16).astype(f32)
        middle = (total - high).astype(bf16).astype(f32)
        low = total - high - middle
        return jnp.where(
            ids == at, high, jnp.where(ids == at + 1, middle, jnp.where(ids == at + 2, low, rest))
        )

    def to_rows(first, second=None):
        ids = lax.broadcasted_iota(jnp.int32, (first.shape[0], 128), 1)
        v = jnp.where(ids == 0, first, 0.0)
        if second is not None:
            v = jnp.where(ids == 1, second, v)
        return dot(e8, v, 1, 1, HI)

    def to_cols(rows):
        return dot(rows, e8, 0, 0, HI)

    def widen(value, extra):
        T[:, 0:C] = value
        return jnp.where(lane >= C, extra, T[...])

    barrier = pltpu.get_barrier_semaphore()
    peers = [dev(y_=add(y, j, 8)) for j in range(1, 8)]
    peers += [dev(z_=add(z, j, 8)) for j in range(1, 8)]
    peers += [dev(y_=add(y, 4, 8), z_=add(z, j, 8)) for j in range(1, 8)]
    peers += [dev(h_=add(h, j, 4)) for j in range(1, 4)]
    peers += [sib, dev(z_=ozh * 4 + zl, c_=oc)]
    for to in peers:
        pl.semaphore_signal(barrier, inc=1, device_id=to, device_id_type=MESH)
    own_w = pltpu.make_async_copy(w, W2.at[c], lsem.at[0])
    own_w.start()
    T[...] = jnp.zeros_like(T)
    for ref in (SB0, SB1, SB2, SB3, SB4):
        ref[...] = jnp.zeros_like(ref)
    PF[...] = jnp.zeros_like(PF)
    two = lax.broadcasted_iota(jnp.int32, (8, 384), 0)
    TW[...] = to_cols(
        jnp.where(two == 0, ids_in[...].astype(f32), jnp.where(two == 1, scale_in[...], 0.0))
    ).reshape(4, 2, R, 128)
    chosen = jnp.concatenate([TW[j, c] for j in range(4)], axis=0)
    targets, weights = pick(chosen, 0), pick(chosen, 1)
    pl.semaphore_wait(barrier, len(peers))

    yq, ym = lax.div(y, 4), lax.rem(y, 4)
    hf = lax.rem(zl, 2)
    in_half = hf == yq
    y_to = add(y, 4 * zh, 8)
    first = jnp.where(in_half, 0, 4)
    y_from = hf * 4 + ym
    a_r = slots(4)
    for kind in range(2):
        for zh_to in range(2):
            z_to = zh_to * 4 + kind * 2 + yq
            send(
                lambda kind=kind: (trunk_in, embed_in)[kind], lambda: XB.at[ym, z],
                0, a_r + zl, dev(y_=y_to, z_=z_to), (z_to != z) | (zh != 0),
            )

            def keep(kind=kind):
                XB[ym, z] = (trunk_in, embed_in)[kind][...]

            pl.when((z_to == z) & (zh == 0))(keep)
    w_s = slots(1)
    send(lambda: w, lambda: W2.at[c], w_s, w_s, sib)

    owner = c == zh
    donor = c != zh
    u_f = slots(1)
    u_x, u_q = some(9, 4)
    u_b, u_d = u_x + 4, u_x + 8
    own_u = lambda: pltpu.make_async_copy(u, UP.at[zh], lsem.at[1])
    pl.when(owner)(lambda: own_u().start())

    def quarter_of(at):
        return pl.ds(pl.multiple_of(at * 512, 512), 512)

    mine = quarter_of(h)
    b_s = slots(32)
    for i in range(5):
        for unit in range(4):
            for way in range(2):
                s = add(y, -i, 8) if way == 0 else add(y, i, 8)
                k = lax.rem(s, 4)
                zs = jnp.where(lax.div(s, 4) == hf, 0, 4) + unit
                idx = b_s + (way * 4 + i) * 4 + unit
                if i == 0 and way == 0:
                    pl.when((zs != z) | (zh != 0))(lambda: recv(XB.at[ym, zs], a_r + unit))
                if i > 0 and (i < 4 or unit // 2 == way):
                    recv(XB.at[k, zs], idx - 4)
                if i < 3 or (i == 3 and unit // 2 == way):
                    send(
                        lambda k=k, zs=zs: XB.at[k, zs], lambda k=k, zs=zs: XB.at[k, zs],
                        idx, idx, right if way == 0 else left,
                    )
        if i == 1:
            send(
                lambda: u.at[:, mine], lambda: UP.at[zh, :, mine], u_d, u_q + h,
                dev(z_=ozh * 4 + zl), donor,
            )

    send(lambda: u, lambda: UP.at[zh], u_f, u_f, sib, owner)
    pl.when(owner)(lambda: recv(UP.at[ozh, :, mine], u_q + h))
    for j in range(1, 4):
        send(
            lambda: UP.at[ozh, :, mine], lambda: UP.at[ozh, :, mine], u_x + j, u_q + h,
            dev(h_=add(h, j, 4)), owner,
        )
    send(lambda: UP.at[ozh, :, mine], lambda: UP.at[ozh, :, mine], u_b, u_q + h, sib, owner)

    own_w.wait()
    recv(W2.at[oc], w_s)
    acc = jnp.zeros((N, C), f32)
    squares = jnp.zeros((N, 1), f32)
    for q in range(8):
        block = XB[q // 2, (q % 2) * 4 : (q % 2) * 4 + 4].reshape(N, C)
        acc = acc + dot(block, W2[q // 4, :, (q % 4) * C : (q % 4 + 1) * C], 1, 1)
        wide = block.astype(f32)
        squares = squares + jnp.sum(wide * wide, axis=1, keepdims=True)
    PF[:, :, 0:C] = acc.reshape(4, R, C)
    lane3 = lax.broadcasted_iota(jnp.int32, (4, R, CP), 2)
    PB[...] = in_three(squares.reshape(4, R, 1), C, lane3, PF[...]).astype(bf16)
    p_s, p_r = some(4, 4)
    for j in range(1, 4):
        zt = add(zl, j, 4)
        send(
            lambda zt=zt: PB.at[zt], lambda: R2.at[zl], p_s + j, p_r + zl, dev(z_=zh * 4 + zt)
        )
    R2[zl] = PB[zl]
    x_s = slots(1)
    send(lambda: XB.at[pl.ds(2 * oc, 2)], lambda: XS, x_s, x_s, sib)
    for j in range(1, 4):
        zt = add(zl, j, 4)
        recv(R2.at[zt], p_r + zt)
    from_trunk = R2[0].astype(f32) + R2[1].astype(f32)
    from_embed = R2[2].astype(f32) + R2[3].astype(f32)
    trunk = trunk_in[...].astype(f32)
    embed = embed_in[...].astype(f32)
    trunk_scale = lax.rsqrt(picks(from_trunk, C, 3) / D + EPS)
    embed_scale = lax.rsqrt(picks(from_embed, C, 3) / D + EPS)
    mixed = trunk + trunk_scale * from_trunk[:, 0:C] + embed_scale * from_embed[:, 0:C]
    MX[...] = mixed
    gains = gain[...].reshape(1, C)
    total = jnp.sum(mixed * mixed, axis=1, keepdims=True)
    pieces = in_three(total, C, lane, jnp.zeros((R, CP), f32))
    Y8[z] = widen(mixed * gains, pieces).astype(bf16)
    y_s, y_r = some(8, 8)
    for j in range(1, 8):
        send(lambda: Y8.at[z], lambda: Y8.at[z], y_s + j, y_r + z, dev(z_=add(z, j, 8)))
    for j in range(1, 4):
        ht = add(h, j, 4)
        quarter = quarter_of(ht)
        pl.when(owner)(lambda: recv(UP.at[ozh, :, quarter], u_q + ht))
        send(
            lambda quarter=quarter: UP.at[ozh, :, quarter], lambda quarter=quarter: UP.at[ozh, :, quarter],
            u_b + j, u_q + ht, sib, owner,
        )
    for j in range(1, 8):
        zs = add(z, j, 8)
        recv(Y8.at[zs], y_r + zs)

    wide = Y8[...].astype(f32)
    split = picks(wide, C, 3)
    part_squares = (split[0:4] + split[4:8]).reshape(N, 1)
    SB0[:, 0:N] = to_rows(part_squares)
    s0_s, s0_r = some(8, 8)
    for j in range(1, 8):
        send(lambda: SB0, lambda: SY0.at[y], s0_s + j, s0_r + y, dev(y_=add(y, j, 8)))
    SY0[y] = SB0[...]

    @pl.when(owner)
    def _():
        own_u().wait()

    @pl.when(donor)
    def _():
        recv(UP.at[zh], u_f)
        for j in range(4):
            recv(UP.at[ozh, :, pl.ds(j * 512, 512)], u_q + j)

    y0 = Y8[0:4].reshape(N, CP)[:, 0:C]
    y1 = Y8[4:8].reshape(N, CP)[:, 0:C]

    def logits_block(at):
        cols = pl.ds(pl.multiple_of(at * VC, VC), VC)
        LP[at] = dot(y0, UP[0, :, cols], 1, 0) + dot(y1, UP[1, :, cols], 1, 0)

    l_s = slots(32)

    def hop(o, way, unit, got):
        to = add(y, o, 8) if way == 0 else add(y, -o, 8)
        rows = slice(unit * R, unit * R + R)
        idx = l_s + (way * 4 + o) * 4 + unit
        if got:
            last = RL2 if (o == 0 and way == 1) else RL.at[to]
            recv(last.at[rows], idx)
            LP[to, rows] = LP[to, rows] + last[rows]
        if o:
            place = RL2 if (o == 1 and way == 1) else RL.at[to]
            send(
                lambda: LP.at[to, rows], lambda: place.at[rows], idx - 4, idx - 4,
                right if way == 0 else left,
            )

    logits_block(add(y, 4, 8))
    for unit in range(2):
        hop(4, 0, unit, False)
        hop(4, 1, unit + 2, False)
    logits_block(add(y, 3, 8))
    logits_block(add(y, -3, 8))
    for unit in range(2):
        hop(3, 0, unit + 2, False)
        hop(3, 1, unit, False)
    logits_block(add(y, 2, 8))
    logits_block(add(y, -2, 8))
    for unit in range(2):
        hop(3, 0, unit, True)
        hop(3, 1, unit + 2, True)
    logits_block(add(y, 1, 8))
    logits_block(add(y, -1, 8))
    logits_block(y)
    for o in (2, 1, 0):
        for unit in (2, 3, 0, 1):
            hop(o, 0, unit, True)
            hop(o, 1, (unit + 2) % 4, True)
    for j in range(1, 8):
        ys = add(y, j, 8)
        recv(SY0.at[ys], s0_r + ys)
    all_squares = to_cols(jnp.sum(SY0[...], axis=0)[:, 0:N])
    mixed_scale = lax.rsqrt(pick(all_squares, 0) / D + EPS)
    MSC[...] = jnp.broadcast_to(mixed_scale, (N, 128)).reshape(4, R, 128)
    YN[0] = (y0.astype(f32) * mixed_scale).astype(bf16)
    YN[1] = (y1.astype(f32) * mixed_scale).astype(bf16)
    n_s = slots(1)
    send(lambda: YN.at[oc], lambda: YS, n_s, n_s, sib)

    logits = LP[y] * mixed_scale
    largest = jnp.max(logits, axis=1, keepdims=True)
    summed = jnp.sum(jnp.exp(logits - largest), axis=1, keepdims=True)
    SB1[:, 0:N] = to_rows(largest, summed)
    s1_s, s1_r = some(8, 8)
    for j in range(1, 8):
        send(lambda: SB1, lambda: SY1.at[y], s1_s + j, s1_r + y, dev(y_=add(y, j, 8)))
    SY1[y] = SB1[...]

    def merge(ref):
        every = ref[...]
        top = jnp.max(every[:, 0:1, :], axis=0)
        whole = jnp.sum(every[:, 1:2, :] * jnp.exp(every[:, 0:1, :] - top[None]), axis=0)
        ids = lax.broadcasted_iota(jnp.int32, (8, VC), 0)
        return jnp.where(ids == 0, top, jnp.where(ids == 1, whole, 0.0))

    for j in range(1, 8):
        ys = add(y, j, 8)
        recv(SY1.at[ys], s1_r + ys)
    SB2[...] = merge(SY1)
    s2_s, s2_r = some(8, 8)
    for j in range(1, 8):
        send(lambda: SB2, lambda: SZ2.at[z], s2_s + j, s2_r + z, dev(z_=add(z, j, 8)))
    SZ2[z] = SB2[...]
    for j in range(1, 8):
        zs = add(z, j, 8)
        recv(SZ2.at[zs], s2_r + zs)
    stats = to_cols(merge(SZ2)[:, 0:N])
    probs = jnp.exp(logits - pick(stats, 0)) / pick(stats, 1)
    vocab_ids = (zl * 4096 + zh * 2048 + y * VC) + lax.broadcasted_iota(jnp.int32, (N, VC), 1)
    hits = (vocab_ids.astype(f32) == targets).astype(f32)
    GA[y] = (weights * (probs - hits)).astype(bf16)

    g_s = slots(32)
    for i in range(5):
        for unit in range(4):
            for way in range(2):
                s = add(y, -i, 8) if way == 0 else add(y, i, 8)
                rows = slice(unit * R, unit * R + R)
                idx = g_s + (way * 4 + i) * 4 + unit
                if i > 0 and (i < 4 or unit // 2 == way):
                    recv(GA.at[s, rows], idx - 4)
                if i < 3 or (i == 3 and unit // 2 == way):
                    send(
                        lambda s=s, rows=rows: GA.at[s, rows], lambda s=s, rows=rows: GA.at[s, rows],
                        idx, idx, right if way == 0 else left,
                    )
    gs_s = slots(1)
    send(lambda: GA, lambda: GS, gs_s, gs_s, sib)

    GN[...] = jnp.zeros_like(GN)

    def normed_block(at, carry):
        rows = pl.ds(pl.multiple_of(at * VC, VC), VC)
        grads = GA[at]
        for zc in range(2):
            GN[zc] += dot(grads, UP[zc, :, rows], 1, 1)
        return carry

    lax.fori_loop(0, 8, normed_block, 0)
    NB[...] = GN[...].astype(bf16).reshape(8, R, C)
    n8_s, n8_r = some(8, 8)
    for j in range(1, 8):
        zt = add(z, j, 8)
        send(lambda zt=zt: NB.at[zt], lambda: NR.at[z], n8_s + j, n8_r + z, dev(z_=zt))
    NR[z] = NB[z]

    held0 = Y8[0:4].reshape(N, CP)[:, 0:C].astype(f32)
    held1 = Y8[4:8].reshape(N, CP)[:, 0:C].astype(f32)
    SB3[:, 0:N] = to_rows(
        jnp.sum(GN[0] * held0, axis=1, keepdims=True) + jnp.sum(GN[1] * held1, axis=1, keepdims=True)
    )
    s3_s, s3_r = some(8, 8)
    for j in range(1, 8):
        send(lambda: SB3, lambda: SY3.at[y], s3_s + j, s3_r + y, dev(y_=add(y, j, 8)))
    SY3[y] = SB3[...]
    for j in range(1, 8):
        ys = add(y, j, 8)
        recv(SY3.at[ys], s3_r + ys)
    SB6[...] = jnp.sum(SY3[...], axis=0)
    s6_s, s6_r = some(8, 8)
    for j in range(1, 8):
        send(lambda: SB6, lambda: SZ6.at[z], s6_s + j, s6_r + z, dev(z_=add(z, j, 8)))
    SZ6[z] = SB6[...]
    for j in range(1, 8):
        zs = add(z, j, 8)
        recv(NR.at[zs], n8_r + zs)
    scaled = jnp.sum(NR[...].astype(f32), axis=0) * gains
    scale_own = MSC[zl][:, 0:1]
    mixed_normed = MX[...] * scale_own
    for j in range(1, 8):
        zs = add(z, j, 8)
        recv(SZ6.at[zs], s6_r + zs)
    INN[...] = to_cols(jnp.sum(SZ6[...], axis=0)[:, 0:N]).reshape(4, R, 128)
    inner = scale_own * pick(INN[zl], 0)
    grad_mixed = scale_own * (scaled - mixed_normed * (inner / D))
    GMF[...] = grad_mixed
    pieces = in_three(trunk_scale, C, lane, in_three(embed_scale, C + 3, lane, jnp.zeros((R, CP), f32)))
    GMB[zl] = widen(grad_mixed, pieces).astype(bf16)
    d_s, d_r = some(4, 4)
    for j in range(1, 4):
        zt = add(zl, j, 4)
        send(lambda: GMB.at[zl], lambda: GMB.at[zl], d_s + j, d_r + zl, dev(z_=zh * 4 + zt))

    recv(GS, gs_s)
    recv(YS, n_s)
    normed_mine = YN[c]
    normed_sib = YS[...]

    def vocab_block(at, carry):
        value = dot(normed_mine, GA[at], 0, 0) + dot(normed_sib, GS[at], 0, 0)
        VB[lax.div(at, 2), :, pl.ds(pl.multiple_of(lax.rem(at, 2) * VC, VC), VC)] = value.astype(bf16)
        return carry

    lax.fori_loop(0, 8, vocab_block, 0)
    v_s, v_r = some(4, 4)
    for j in range(1, 4):
        ht = add(h, j, 4)
        send(lambda ht=ht: VB.at[ht], lambda: VR.at[h], v_s + j, v_r + h, dev(h_=ht))
    VR[h] = VB[h]

    for j in range(1, 4):
        zs = add(zl, j, 4)
        recv(GMB.at[zs], d_r + zs)
    gathered = GMB[...].reshape(N, CP)
    grad_low = gathered[:, 0:C]
    joined_scale = picks(gathered.astype(f32), C + 3 * lax.div(zl, 2), 3)
    grad_joined = (grad_low.astype(f32) * joined_scale).astype(bf16)
    GML[...] = grad_joined
    c_s = slots(1)
    send(lambda: GML, lambda: GMS, c_s, c_s, sib)

    for q in range(8):
        value = dot(grad_low, W2[q // 4, :, (q % 4) * C : (q % 4 + 1) * C], 1, 0)
        JP[q // 2, (q % 2) * 4 : (q % 2) * 4 + 4] = value.astype(bf16).reshape(4, R, C)
    q_s = slots(1)

    def sum_vocab():
        for j in range(1, 4):
            hs = add(h, j, 4)
            recv(VR.at[hs], v_r + hs)
        vocab_total = jnp.sum(VR[...].astype(f32), axis=0)
        ug[...] = vocab_total
        VSB[...] = vocab_total.astype(bf16)
        send(lambda: VSB, lambda: VSR, q_s, q_s, dev(z_=ozh * 4 + zl, c_=oc), donor)

    j_s = slots(32)

    def grad_hop(o, way, unit, got):
        to = add(y, o, 8) if way == 0 else add(y, -o, 8)
        k = lax.rem(to, 4)
        part = jnp.where(lax.div(to, 4) == hf, 0, 4) + unit
        idx = j_s + (way * 4 + o) * 4 + unit
        if got:
            last = RJ2.at[unit] if (o == 0 and way == 1) else RJ.at[k, part]
            recv(last, idx)
            JP[k, part] = (JP[k, part].astype(f32) + last[...].astype(f32)).astype(bf16)
        if o:
            place = RJ2.at[unit] if (o == 1 and way == 1) else RJ.at[k, part]
            send(
                lambda: JP.at[k, part], lambda: place, idx - 4, idx - 4,
                right if way == 0 else left,
            )

    for unit in range(2):
        grad_hop(4, 0, unit, False)
        grad_hop(4, 1, unit + 2, False)
    for unit in range(2):
        grad_hop(3, 0, unit + 2, False)
        grad_hop(3, 1, unit, False)
    for unit in range(2):
        grad_hop(3, 0, unit, True)
        grad_hop(3, 1, unit + 2, True)
    for o in (2, 1, 0):
        for unit in (2, 3, 0, 1):
            grad_hop(o, 0, unit, True)
            grad_hop(o, 1, (unit + 2) % 4, True)
        if o == 1:
            sum_vocab()
    kind_mine = lax.div(zl, 2)
    k_r = slots(4)
    for part in range(4):
        z_to = first + part
        send(
            lambda z_to=z_to: JP.at[ym, z_to], lambda: SD.at[kind_mine, zh], 0,
            k_r + kind_mine * 2 + zh, dev(y_=y_from, z_=z_to), jnp.logical_not(in_half & (z_to == z)),
        )

    held = pl.ds(first, 4)
    raw = jnp.sum(JP[ym, held].astype(f32) * XB[ym, held].astype(f32), axis=2, keepdims=True)
    SB4[:, 0:N] = to_rows(raw.reshape(N, 1))
    s4_s, s4_r = some(8, 8)
    for j in range(1, 8):
        send(lambda: SB4, lambda: SY4.at[y], s4_s + j, s4_r + y, dev(y_=add(y, j, 8)))
    SY4[y] = SB4[...]

    @pl.when(in_half & (zh == 0))
    def _():
        SD[kind_mine, zh] = JP[ym, z]

    recv(GMS, c_s)
    recv(XS, x_s)
    grad_sib = GMS[...]
    for kk in range(2):
        for zz in range(2):
            q = kk * 2 + zz
            part = pl.ds(zz * 4, 4)
            cg[:, q * C : (q + 1) * C] = dot(
                grad_joined, XB[2 * c + kk, part].reshape(N, C), 0, 0
            ) + dot(grad_sib, XS[kk, part].reshape(N, C), 0, 0)

    put(2).start()
    for j in range(1, 8):
        ys = add(y, j, 8)
        recv(SY4.at[ys], s4_r + ys)
    SB5[...] = jnp.sum(SY4[...], axis=0)
    s5_s, s5_r = some(8, 8)
    for j in range(1, 8):
        send(lambda: SB5, lambda: SZ5.at[z], s5_s + j, s5_r + z, dev(z_=add(z, j, 8)))
    SZ5[z] = SB5[...]
    for kind in range(2):
        for zs in range(2):
            z_from = zs * 4 + kind * 2 + yq
            pl.when((z_from != z) | (zh != 0))(lambda: recv(SD.at[kind, zs], k_r + kind * 2 + zs))
    trunk_side = SD[0, 0].astype(f32) + SD[0, 1].astype(f32)
    embed_side = SD[1, 0].astype(f32) + SD[1, 1].astype(f32)
    trunk_normed = trunk * trunk_scale
    embed_normed = embed * embed_scale
    before = GMF[...] + trunk_scale * trunk_side
    PRE[...] = before.astype(bf16)
    o_s, o_r = some(4, 4)
    for j in range(1, 4):
        send(lambda: PRE, lambda: XPR.at[h], o_s + j, o_r + h, dev(h_=add(h, j, 4)))
    XPR[h] = PRE[...]
    for j in range(1, 8):
        zs = add(z, j, 8)
        recv(SZ5.at[zs], s5_r + zs)
    ids = lax.broadcasted_iota(jnp.int32, (8, VC), 0)
    SB7[...] = jnp.where(
        ids == 0,
        (SZ5[0] + SZ5[1] + SZ5[4] + SZ5[5])[0:1],
        jnp.where(ids == 1, (SZ5[2] + SZ5[3] + SZ5[6] + SZ5[7])[0:1], 0.0),
    )
    s7_s, s7_r = some(4, 4)
    for j in range(1, 4):
        send(lambda: SB7, lambda: S7.at[h], s7_s + j, s7_r + h, dev(h_=add(h, j, 4)))
    S7[h] = SB7[...]
    pl.when(owner)(lambda: put(3).start())
    for j in range(1, 4):
        hs = add(h, j, 4)
        recv(S7.at[hs], s7_r + hs)
    INN[...] = to_cols(
        jnp.where(ids == 0, jnp.sum(S7[...], axis=0), S7[h])[:, 0:N]
    ).reshape(4, R, 128)
    dots = INN[zl]
    eg[...] = embed_scale * (embed_side - embed_normed * (embed_scale * pick(dots, 1) / D))
    put(1).start()
    for j in range(1, 4):
        hs = add(h, j, 4)
        recv(XPR.at[hs], o_r + hs)
    tg[...] = jnp.sum(XPR[...].astype(f32), axis=0) - trunk_scale * trunk_normed * (
        trunk_scale * pick(dots, 0) / D
    )

    put(0).start()

    @pl.when(donor)
    def _():
        recv(VSR, q_s)
        ug[...] = VSR[...].astype(f32)
        put(3).start()

    for at in range(4):
        put(at).wait()
    assert counts["r"] <= SEMS
    for cond, body in finals[-POOL:]:
        when(cond, body)


def put_out(*refs):
    into, out, held, sems = refs[:4], refs[4:8], refs[8:12], refs[12]
    reads = [pltpu.make_async_copy(into[k], held[k], sems.at[k]) for k in range(4)]
    writes = [pltpu.make_async_copy(held[k], out[k], sems.at[k + 4]) for k in range(4)]
    order = (2, 3, 0, 1)
    for k in order:
        reads[k].start()
    for k in order:
        reads[k].wait()
        writes[k].start()
    for k in order:
        writes[k].wait()


def local(
    trunk_hidden, next_embeds, combine_weight, final_gain, unembed_weight, target_ids, loss_scale
):
    vm = lambda *shape: pltpu.VMEM(shape, f32)
    vb = lambda *shape: pltpu.VMEM(shape, bf16)
    scratch = [
        vm(R, C), vm(R, C), vm(C, 1280), vm(C, 512),
        vb(2, C, 1280), vb(4, 8, R, C), vb(2, 8, R, C), vm(4, R, CP), vb(4, R, CP), vb(4, R, CP), vm(R, CP),
        vb(8, R, CP), vm(R, C), vb(2, C, V), vm(8, N, VC), vm(8, N, VC), vm(4, R, 128),
        vb(2, N, C), vb(N, C),
        vm(8, VC), vm(8, 8, VC), vm(8, VC), vm(8, 8, VC), vm(8, VC), vm(8, 8, VC),
        vb(8, N, VC), vb(8, N, VC), vm(2, N, C), vb(8, R, C), vb(8, R, C),
        vm(4, R, 128), vm(8, VC), vm(8, 8, VC), vm(8, VC), vm(8, 8, VC),
        vm(N, VC), vm(4, 2, R, 128),
        vm(R, C), vb(4, R, CP), vb(N, C), vb(N, C),
        vb(4, 8, R, C), vb(4, 8, R, C), vb(4, R, C), vb(2, 2, R, C),
        vb(R, C), vb(4, R, C), vm(8, VC), vm(8, 8, VC), vm(8, VC), vm(8, 8, VC),
        vm(8, VC), vm(4, 8, VC),
        vb(4, C, 512), vb(4, C, 512), vb(C, 512), vb(C, 512),
        pltpu.SemaphoreType.DMA((POOL,)), pltpu.SemaphoreType.DMA((SEMS,)), pltpu.SemaphoreType.DMA((6,)),
    ]
    spec = pl.BlockSpec(memory_space=pltpu.VMEM)
    remote = pl.BlockSpec(memory_space=pl.ANY)
    trunk_grad, embed_grad, combine_grad, unembed_grad = pl.pallas_call(
        kernel,
        out_shape=(
            jax.ShapeDtypeStruct((R, C), f32),
            jax.ShapeDtypeStruct((R, C), f32),
            jax.ShapeDtypeStruct((C, 1280), f32),
            jax.ShapeDtypeStruct((C, 512), f32),
        ),
        in_specs=[spec, spec, remote, remote, spec, spec, spec],
        out_specs=(remote,) * 4,
        scratch_shapes=scratch,
        compiler_params=pltpu.CompilerParams(
            collective_id=0, has_side_effects=True, vmem_limit_bytes=60 * 1024 * 1024
        ),
    )(
        trunk_hidden,
        next_embeds[0],
        combine_weight[0].T,
        unembed_weight.T,
        final_gain,
        target_ids,
        loss_scale,
    )
    results = (trunk_grad, embed_grad, combine_grad, unembed_grad)
    trunk_grad, embed_grad, combine_grad, unembed_grad = pl.pallas_call(
        put_out,
        out_shape=tuple(jax.ShapeDtypeStruct(r.shape, r.dtype) for r in results),
        in_specs=[remote] * 4,
        out_specs=(remote,) * 4,
        scratch_shapes=[pltpu.VMEM(r.shape, r.dtype) for r in results]
        + [pltpu.SemaphoreType.DMA((8,))],
        compiler_params=pltpu.CompilerParams(vmem_limit_bytes=60 * 1024 * 1024),
    )(*results)
    return trunk_grad, embed_grad[None], combine_grad.T[None], unembed_grad.T[None, None]


def solution(mesh):
    in_specs = (
        P("dp", "tensor"),
        P("head", "dp", "tensor"),
        P("head", "dp", "tensor"),
        P("tensor"),
        P("dp", "tensor"),
        P("head", None),
        P("head", None),
    )
    out_specs = (
        P("dp", "tensor"),
        P("head", "dp", "tensor"),
        P("head", "dp", "tensor"),
        P("dp", "head", None, "tensor"),
    )
    return jax.shard_map(local, mesh=mesh, in_specs=in_specs, out_specs=out_specs, check_vma=False)
```

```python
import jax
import jax.numpy as jnp
from jax import lax
from jax.experimental import pallas as pl
from jax.experimental.pallas import tpu as pltpu
from jax.sharding import PartitionSpec as P

D = 5120
EPS = 1e-05
R = 48
N = 192
C = 320
CP = 384
V = 2048
VC = 256
MESH = pl.DeviceIdType.MESH
HI = lax.Precision.HIGHEST
POOL = 64
SEMS = 246
f32 = jnp.float32
bf16 = jnp.bfloat16


def dot(left, right, a, b, precision=None):
    return lax.dot_general(
        left, right, (((a,), (b,)), ((), ())), precision=precision, preferred_element_type=f32
    )


def kernel(
    trunk_in, embed_in, w, u, gain, ids_in, scale_in,
    tg_out, eg_out, cg_out, ug_out,
    tg, eg, cg, ug,
    W2, XB, XS, PF, PB, R2, T, Y8, MX, UP, LP, RL, MSC, YN, YS,
    SB0, SY0, SB1, SY1, SB2, SZ2, GA, GS, GN, NB, NR, INN, SB3, SY3, SB6, SZ6, RL2, TW,
    GMF, GMB, GML, GMS, JP, RJ, RJ2, SD, PRE, XPR, SB4, SY4, SB5, SZ5, SB7, S7, VB, VR, VSB, VSR,
    ssem, rsem, lsem,
):
    h = lax.axis_index("head")
    t = lax.axis_index("tensor")
    d = lax.axis_index("dp")
    y, zh = lax.div(t, 2), lax.rem(t, 2)
    zl, c = lax.div(d, 2), lax.rem(d, 2)
    z = zh * 4 + zl
    oc, ozh = 1 - c, 1 - zh

    def dev(h_=None, y_=None, z_=None, c_=None):
        h_ = h if h_ is None else h_
        y_ = y if y_ is None else y_
        z_ = z if z_ is None else z_
        c_ = c if c_ is None else c_
        return (h_, y_ * 2 + lax.div(z_, 4), lax.rem(z_, 4) * 2 + c_)

    def add(value, step, size):
        return lax.rem(value + (step + size), size)

    sib = dev(c_=oc)
    right, left = dev(y_=add(y, 1, 8)), dev(y_=add(y, -1, 8))
    me = dev()

    counts = {"r": 0}

    def slots(n):
        first = counts["r"]
        counts["r"] += n
        return first

    def some(sends, receives):
        return 0, slots(receives)

    finals = []

    def copy(src, dst, s, r, to):
        return pltpu.make_async_remote_copy(
            src_ref=src, dst_ref=dst, send_sem=ssem.at[s], recv_sem=rsem.at[r],
            device_id=to, device_id_type=MESH,
        )

    def when(cond, body):
        if cond is None:
            body()
        else:
            pl.when(cond)(body)

    def send(src, dst, s, r, to, cond=None):
        at = len(finals) % POOL
        if len(finals) >= POOL:
            when(*finals[-POOL])
        when(cond, lambda: copy(src(), dst(), at, r, to).start())
        finals.append((cond, lambda: copy(src(), dst(), at, r, to).wait_send()))

    def recv(dst, r):
        copy(dst, dst, 0, r, me).wait_recv()

    def put(at):
        pairs = ((tg, tg_out), (eg, eg_out), (cg, cg_out), (ug, ug_out))
        return pltpu.make_async_copy(*pairs[at], lsem.at[2 + at])

    lane = lax.broadcasted_iota(jnp.int32, (R, CP), 1)
    e8 = (
        lax.broadcasted_iota(jnp.int32, (8, 128), 0) == lax.broadcasted_iota(jnp.int32, (8, 128), 1)
    ).astype(f32)

    def pick(x, at):
        ids = lax.broadcasted_iota(jnp.int32, x.shape, x.ndim - 1)
        return jnp.sum(jnp.where(ids == at, x, 0.0), axis=-1, keepdims=True)

    def picks(x, at, n):
        ids = lax.broadcasted_iota(jnp.int32, x.shape, x.ndim - 1)
        return jnp.sum(jnp.where((ids >= at) & (ids < at + n), x, 0.0), axis=-1, keepdims=True)

    def in_three(total, at, ids, rest):
        high = total.astype(bf16).astype(f32)
        middle = (total - high).astype(bf16).astype(f32)
        low = total - high - middle
        return jnp.where(
            ids == at, high, jnp.where(ids == at + 1, middle, jnp.where(ids == at + 2, low, rest))
        )

    def to_rows(first, second=None):
        ids = lax.broadcasted_iota(jnp.int32, (first.shape[0], 128), 1)
        v = jnp.where(ids == 0, first, 0.0)
        if second is not None:
            v = jnp.where(ids == 1, second, v)
        return dot(e8, v, 1, 1, HI)

    def to_cols(rows):
        return dot(rows, e8, 0, 0, HI)

    def widen(value, extra):
        T[:, 0:C] = value
        return jnp.where(lane >= C, extra, T[...])

    barrier = pltpu.get_barrier_semaphore()
    peers = [dev(y_=add(y, j, 8)) for j in range(1, 8)]
    peers += [dev(z_=add(z, j, 8)) for j in range(1, 8)]
    peers += [dev(y_=add(y, 4, 8), z_=add(z, j, 8)) for j in range(1, 8)]
    peers += [dev(h_=add(h, j, 4)) for j in range(1, 4)]
    peers += [sib, dev(z_=ozh * 4 + zl, c_=oc)]
    for to in peers:
        pl.semaphore_signal(barrier, inc=1, device_id=to, device_id_type=MESH)
    own_w = pltpu.make_async_copy(w, W2.at[c], lsem.at[0])
    own_w.start()
    T[...] = jnp.zeros_like(T)
    for ref in (SB0, SB1, SB2, SB3, SB4):
        ref[...] = jnp.zeros_like(ref)
    PF[...] = jnp.zeros_like(PF)
    two = lax.broadcasted_iota(jnp.int32, (8, 384), 0)
    TW[...] = to_cols(
        jnp.where(two == 0, ids_in[...].astype(f32), jnp.where(two == 1, scale_in[...], 0.0))
    ).reshape(4, 2, R, 128)
    chosen = jnp.concatenate([TW[j, c] for j in range(4)], axis=0)
    targets, weights = pick(chosen, 0), pick(chosen, 1)
    pl.semaphore_wait(barrier, len(peers))

    yq, ym = lax.div(y, 4), lax.rem(y, 4)
    hf = lax.rem(zl, 2)
    in_half = hf == yq
    y_to = add(y, 4 * zh, 8)
    first = jnp.where(in_half, 0, 4)
    y_from = hf * 4 + ym
    a_r = slots(4)
    for kind in range(2):
        for zh_to in range(2):
            z_to = zh_to * 4 + kind * 2 + yq
            send(
                lambda kind=kind: (trunk_in, embed_in)[kind], lambda: XB.at[ym, z],
                0, a_r + zl, dev(y_=y_to, z_=z_to), (z_to != z) | (zh != 0),
            )

            def keep(kind=kind):
                XB[ym, z] = (trunk_in, embed_in)[kind][...]

            pl.when((z_to == z) & (zh == 0))(keep)
    w_s = slots(1)
    send(lambda: w, lambda: W2.at[c], w_s, w_s, sib)

    owner = c == zh
    donor = c != zh
    u_f = slots(1)
    u_x, u_q = some(9, 4)
    u_b, u_d = u_x + 4, u_x + 8
    send(lambda: u, lambda: UP.at[zh], u_f, u_f, sib, owner)
    own_u = lambda: pltpu.make_async_copy(u, UP.at[zh], lsem.at[1])
    pl.when(owner)(lambda: own_u().start())

    def quarter_of(at):
        return pl.ds(pl.multiple_of(at * 512, 512), 512)

    mine = quarter_of(h)
    b_s = slots(32)
    for i in range(5):
        for unit in range(4):
            for way in range(2):
                s = add(y, -i, 8) if way == 0 else add(y, i, 8)
                k = lax.rem(s, 4)
                zs = jnp.where(lax.div(s, 4) == hf, 0, 4) + unit
                idx = b_s + (way * 4 + i) * 4 + unit
                if i == 0 and way == 0:
                    pl.when((zs != z) | (zh != 0))(lambda: recv(XB.at[ym, zs], a_r + unit))
                if i > 0 and (i < 4 or unit // 2 == way):
                    recv(XB.at[k, zs], idx - 4)
                if i < 3 or (i == 3 and unit // 2 == way):
                    send(
                        lambda k=k, zs=zs: XB.at[k, zs], lambda k=k, zs=zs: XB.at[k, zs],
                        idx, idx, right if way == 0 else left,
                    )
        if i == 0:
            send(
                lambda: u.at[:, mine], lambda: UP.at[zh, :, mine], u_d, u_q + h,
                dev(z_=ozh * 4 + zl), donor,
            )
        if i == 3:
            pl.when(owner)(lambda: recv(UP.at[ozh, :, mine], u_q + h))
            for j in range(1, 4):
                send(
                    lambda: UP.at[ozh, :, mine], lambda: UP.at[ozh, :, mine], u_x + j, u_q + h,
                    dev(h_=add(h, j, 4)), owner,
                )
            send(lambda: UP.at[ozh, :, mine], lambda: UP.at[ozh, :, mine], u_b, u_q + h, sib, owner)

    own_w.wait()
    recv(W2.at[oc], w_s)
    acc = jnp.zeros((N, C), f32)
    squares = jnp.zeros((N, 1), f32)
    for q in range(8):
        block = XB[q // 2, (q % 2) * 4 : (q % 2) * 4 + 4].reshape(N, C)
        acc = acc + dot(block, W2[q // 4, :, (q % 4) * C : (q % 4 + 1) * C], 1, 1)
        wide = block.astype(f32)
        squares = squares + jnp.sum(wide * wide, axis=1, keepdims=True)
    PF[:, :, 0:C] = acc.reshape(4, R, C)
    lane3 = lax.broadcasted_iota(jnp.int32, (4, R, CP), 2)
    PB[...] = in_three(squares.reshape(4, R, 1), C, lane3, PF[...]).astype(bf16)
    p_s, p_r = some(4, 4)
    for j in range(1, 4):
        zt = add(zl, j, 4)
        send(
            lambda zt=zt: PB.at[zt], lambda: R2.at[zl], p_s + j, p_r + zl, dev(z_=zh * 4 + zt)
        )
    R2[zl] = PB[zl]
    for j in range(1, 4):
        zt = add(zl, j, 4)
        recv(R2.at[zt], p_r + zt)
    from_trunk = R2[0].astype(f32) + R2[1].astype(f32)
    from_embed = R2[2].astype(f32) + R2[3].astype(f32)
    trunk = trunk_in[...].astype(f32)
    embed = embed_in[...].astype(f32)
    trunk_scale = lax.rsqrt(picks(from_trunk, C, 3) / D + EPS)
    embed_scale = lax.rsqrt(picks(from_embed, C, 3) / D + EPS)
    mixed = trunk + trunk_scale * from_trunk[:, 0:C] + embed_scale * from_embed[:, 0:C]
    MX[...] = mixed
    gains = gain[...].reshape(1, C)
    total = jnp.sum(mixed * mixed, axis=1, keepdims=True)
    pieces = in_three(total, C, lane, jnp.zeros((R, CP), f32))
    Y8[z] = widen(mixed * gains, pieces).astype(bf16)
    y_s, y_r = some(8, 8)
    for j in range(1, 8):
        send(lambda: Y8.at[z], lambda: Y8.at[z], y_s + j, y_r + z, dev(z_=add(z, j, 8)))
    for j in range(1, 4):
        ht = add(h, j, 4)
        quarter = quarter_of(ht)
        pl.when(owner)(lambda: recv(UP.at[ozh, :, quarter], u_q + ht))
        send(
            lambda quarter=quarter: UP.at[ozh, :, quarter], lambda quarter=quarter: UP.at[ozh, :, quarter],
            u_b + j, u_q + ht, sib, owner,
        )
    for j in range(1, 8):
        zs = add(z, j, 8)
        recv(Y8.at[zs], y_r + zs)

    x_s = slots(1)
    send(lambda: XB.at[pl.ds(2 * oc, 2)], lambda: XS, x_s, x_s, sib)

    wide = Y8[...].astype(f32)
    split = picks(wide, C, 3)
    part_squares = (split[0:4] + split[4:8]).reshape(N, 1)
    SB0[:, 0:N] = to_rows(part_squares)
    s0_s, s0_r = some(8, 8)
    for j in range(1, 8):
        send(lambda: SB0, lambda: SY0.at[y], s0_s + j, s0_r + y, dev(y_=add(y, j, 8)))
    SY0[y] = SB0[...]

    @pl.when(owner)
    def _():
        own_u().wait()

    @pl.when(donor)
    def _():
        recv(UP.at[zh], u_f)
        for j in range(4):
            recv(UP.at[ozh, :, pl.ds(j * 512, 512)], u_q + j)

    y0 = Y8[0:4].reshape(N, CP)[:, 0:C]
    y1 = Y8[4:8].reshape(N, CP)[:, 0:C]

    def logits_block(at):
        cols = pl.ds(pl.multiple_of(at * VC, VC), VC)
        LP[at] = dot(y0, UP[0, :, cols], 1, 0) + dot(y1, UP[1, :, cols], 1, 0)

    l_s = slots(32)

    def hop(o, way, unit, got):
        to = add(y, o, 8) if way == 0 else add(y, -o, 8)
        rows = slice(unit * R, unit * R + R)
        idx = l_s + (way * 4 + o) * 4 + unit
        if got:
            last = RL2 if (o == 0 and way == 1) else RL.at[to]
            recv(last.at[rows], idx)
            LP[to, rows] = LP[to, rows] + last[rows]
        if o:
            place = RL2 if (o == 1 and way == 1) else RL.at[to]
            send(
                lambda: LP.at[to, rows], lambda: place.at[rows], idx - 4, idx - 4,
                right if way == 0 else left,
            )

    logits_block(add(y, 4, 8))
    for unit in range(2):
        hop(4, 0, unit, False)
        hop(4, 1, unit + 2, False)
    logits_block(add(y, 3, 8))
    logits_block(add(y, -3, 8))
    for unit in range(2):
        hop(3, 0, unit + 2, False)
        hop(3, 1, unit, False)
    logits_block(add(y, 2, 8))
    logits_block(add(y, -2, 8))
    for unit in range(2):
        hop(3, 0, unit, True)
        hop(3, 1, unit + 2, True)
    logits_block(add(y, 1, 8))
    logits_block(add(y, -1, 8))
    logits_block(y)
    for o in (2, 1, 0):
        for unit in (2, 3, 0, 1):
            hop(o, 0, unit, True)
            hop(o, 1, (unit + 2) % 4, True)
    for j in range(1, 8):
        ys = add(y, j, 8)
        recv(SY0.at[ys], s0_r + ys)
    all_squares = to_cols(jnp.sum(SY0[...], axis=0)[:, 0:N])
    mixed_scale = lax.rsqrt(pick(all_squares, 0) / D + EPS)
    MSC[...] = jnp.broadcast_to(mixed_scale, (N, 128)).reshape(4, R, 128)
    YN[0] = (y0.astype(f32) * mixed_scale).astype(bf16)
    YN[1] = (y1.astype(f32) * mixed_scale).astype(bf16)
    n_s = slots(1)
    send(lambda: YN.at[oc], lambda: YS, n_s, n_s, sib)

    logits = LP[y] * mixed_scale
    largest = jnp.max(logits, axis=1, keepdims=True)
    summed = jnp.sum(jnp.exp(logits - largest), axis=1, keepdims=True)
    SB1[:, 0:N] = to_rows(largest, summed)
    s1_s, s1_r = some(8, 8)
    for j in range(1, 8):
        send(lambda: SB1, lambda: SY1.at[y], s1_s + j, s1_r + y, dev(y_=add(y, j, 8)))
    SY1[y] = SB1[...]

    def merge(ref):
        every = ref[...]
        top = jnp.max(every[:, 0:1, :], axis=0)
        whole = jnp.sum(every[:, 1:2, :] * jnp.exp(every[:, 0:1, :] - top[None]), axis=0)
        ids = lax.broadcasted_iota(jnp.int32, (8, VC), 0)
        return jnp.where(ids == 0, top, jnp.where(ids == 1, whole, 0.0))

    for j in range(1, 8):
        ys = add(y, j, 8)
        recv(SY1.at[ys], s1_r + ys)
    SB2[...] = merge(SY1)
    s2_s, s2_r = some(8, 8)
    for j in range(1, 8):
        send(lambda: SB2, lambda: SZ2.at[z], s2_s + j, s2_r + z, dev(z_=add(z, j, 8)))
    SZ2[z] = SB2[...]
    for j in range(1, 8):
        zs = add(z, j, 8)
        recv(SZ2.at[zs], s2_r + zs)
    stats = to_cols(merge(SZ2)[:, 0:N])
    probs = jnp.exp(logits - pick(stats, 0)) / pick(stats, 1)
    vocab_ids = (zl * 4096 + zh * 2048 + y * VC) + lax.broadcasted_iota(jnp.int32, (N, VC), 1)
    hits = (vocab_ids.astype(f32) == targets).astype(f32)
    GA[y] = (weights * (probs - hits)).astype(bf16)

    def normed_block(at, fresh=False):
        rows = pl.ds(pl.multiple_of(at * VC, VC), VC)
        grads = GA[at]
        for zc in range(2):
            value = dot(grads, UP[zc, :, rows], 1, 1)
            GN[zc] = value if fresh else GN[zc] + value

    gs_s = slots(8)

    def to_sibling(at):
        send(lambda: GA.at[at], lambda: GS.at[at], 0, gs_s + at, sib)

    g_s = slots(32)
    for i in range(5):
        for unit in range(4):
            for way in range(2):
                s = add(y, -i, 8) if way == 0 else add(y, i, 8)
                rows = slice(unit * R, unit * R + R)
                idx = g_s + (way * 4 + i) * 4 + unit
                if i > 0 and (i < 4 or unit // 2 == way):
                    recv(GA.at[s, rows], idx - 4)
                if i < 3 or (i == 3 and unit // 2 == way):
                    send(
                        lambda s=s, rows=rows: GA.at[s, rows], lambda s=s, rows=rows: GA.at[s, rows],
                        idx, idx, right if way == 0 else left,
                    )
        arrived = {0: (y,), 4: (add(y, 4, 8),)}.get(i, (add(y, -i, 8), add(y, i, 8)))
        for at in arrived:
            to_sibling(at)
        for at in arrived:
            normed_block(at, i == 0)

    NB[...] = GN[...].astype(bf16).reshape(8, R, C)
    n8_s, n8_r = some(8, 8)
    for j in range(1, 8):
        zt = add(z, j, 8)
        send(lambda zt=zt: NB.at[zt], lambda: NR.at[z], n8_s + j, n8_r + z, dev(z_=zt))
    NR[z] = NB[z]

    held0 = Y8[0:4].reshape(N, CP)[:, 0:C].astype(f32)
    held1 = Y8[4:8].reshape(N, CP)[:, 0:C].astype(f32)
    SB3[:, 0:N] = to_rows(
        jnp.sum(GN[0] * held0, axis=1, keepdims=True) + jnp.sum(GN[1] * held1, axis=1, keepdims=True)
    )
    s3_s, s3_r = some(8, 8)
    for j in range(1, 8):
        send(lambda: SB3, lambda: SY3.at[y], s3_s + j, s3_r + y, dev(y_=add(y, j, 8)))
    SY3[y] = SB3[...]
    for j in range(1, 8):
        ys = add(y, j, 8)
        recv(SY3.at[ys], s3_r + ys)
    SB6[...] = jnp.sum(SY3[...], axis=0)
    s6_s, s6_r = some(8, 8)
    for j in range(1, 8):
        send(lambda: SB6, lambda: SZ6.at[z], s6_s + j, s6_r + z, dev(z_=add(z, j, 8)))
    SZ6[z] = SB6[...]

    for j in range(8):
        recv(GS.at[j], gs_s + j)
    recv(YS, n_s)
    normed_mine = YN[c]
    normed_sib = YS[...]

    def vocab_block(at, carry):
        value = dot(normed_mine, GA[at], 0, 0) + dot(normed_sib, GS[at], 0, 0)
        VB[lax.div(at, 2), :, pl.ds(pl.multiple_of(lax.rem(at, 2) * VC, VC), VC)] = value.astype(bf16)
        return carry

    lax.fori_loop(0, 8, vocab_block, 0)
    v_s, v_r = some(4, 4)
    for j in range(1, 4):
        ht = add(h, j, 4)
        send(lambda ht=ht: VB.at[ht], lambda: VR.at[h], v_s + j, v_r + h, dev(h_=ht))
    VR[h] = VB[h]

    for j in range(1, 8):
        zs = add(z, j, 8)
        recv(NR.at[zs], n8_r + zs)
    scaled = jnp.sum(NR[...].astype(f32), axis=0) * gains
    scale_own = MSC[zl][:, 0:1]
    mixed_normed = MX[...] * scale_own
    for j in range(1, 8):
        zs = add(z, j, 8)
        recv(SZ6.at[zs], s6_r + zs)
    INN[...] = to_cols(jnp.sum(SZ6[...], axis=0)[:, 0:N]).reshape(4, R, 128)
    inner = scale_own * pick(INN[zl], 0)
    grad_mixed = scale_own * (scaled - mixed_normed * (inner / D))
    GMF[...] = grad_mixed
    pieces = in_three(trunk_scale, C, lane, in_three(embed_scale, C + 3, lane, jnp.zeros((R, CP), f32)))
    GMB[zl] = widen(grad_mixed, pieces).astype(bf16)
    d_s, d_r = some(4, 4)
    for j in range(1, 4):
        zt = add(zl, j, 4)
        send(lambda: GMB.at[zl], lambda: GMB.at[zl], d_s + j, d_r + zl, dev(z_=zh * 4 + zt))

    for j in range(1, 4):
        zs = add(zl, j, 4)
        recv(GMB.at[zs], d_r + zs)
    gathered = GMB[...].reshape(N, CP)
    grad_low = gathered[:, 0:C]
    joined_scale = picks(gathered.astype(f32), C + 3 * lax.div(zl, 2), 3)
    grad_joined = (grad_low.astype(f32) * joined_scale).astype(bf16)
    GML[...] = grad_joined
    c_s = slots(1)
    send(lambda: GML, lambda: GMS, c_s, c_s, sib)

    for q in range(8):
        value = dot(grad_low, W2[q // 4, :, (q % 4) * C : (q % 4 + 1) * C], 1, 0)
        JP[q // 2, (q % 2) * 4 : (q % 2) * 4 + 4] = value.astype(bf16).reshape(4, R, C)
    q_s = slots(1)

    def sum_vocab():
        for j in range(1, 4):
            hs = add(h, j, 4)
            recv(VR.at[hs], v_r + hs)
        vocab_total = jnp.sum(VR[...].astype(f32), axis=0)
        ug[...] = vocab_total
        VSB[...] = vocab_total.astype(bf16)
        send(lambda: VSB, lambda: VSR, q_s, q_s, dev(z_=ozh * 4 + zl, c_=oc), donor)

    j_s = slots(32)

    def grad_hop(o, way, unit, got):
        to = add(y, o, 8) if way == 0 else add(y, -o, 8)
        k = lax.rem(to, 4)
        part = jnp.where(lax.div(to, 4) == hf, 0, 4) + unit
        idx = j_s + (way * 4 + o) * 4 + unit
        if got:
            last = RJ2.at[unit] if (o == 0 and way == 1) else RJ.at[k, part]
            recv(last, idx)
            JP[k, part] = (JP[k, part].astype(f32) + last[...].astype(f32)).astype(bf16)
        if o:
            place = RJ2.at[unit] if (o == 1 and way == 1) else RJ.at[k, part]
            send(
                lambda: JP.at[k, part], lambda: place, idx - 4, idx - 4,
                right if way == 0 else left,
            )

    for unit in range(2):
        grad_hop(4, 0, unit, False)
        grad_hop(4, 1, unit + 2, False)
    for unit in range(2):
        grad_hop(3, 0, unit + 2, False)
        grad_hop(3, 1, unit, False)
    for unit in range(2):
        grad_hop(3, 0, unit, True)
        grad_hop(3, 1, unit + 2, True)
    for o in (2, 1, 0):
        for unit in (2, 3, 0, 1):
            grad_hop(o, 0, unit, True)
            grad_hop(o, 1, (unit + 2) % 4, True)
        if o == 2:
            sum_vocab()
    kind_mine = lax.div(zl, 2)
    k_r = slots(4)
    for part in range(4):
        z_to = first + part
        send(
            lambda z_to=z_to: JP.at[ym, z_to], lambda: SD.at[kind_mine, zh], 0,
            k_r + kind_mine * 2 + zh, dev(y_=y_from, z_=z_to), jnp.logical_not(in_half & (z_to == z)),
        )

    held = pl.ds(first, 4)
    raw = jnp.sum(JP[ym, held].astype(f32) * XB[ym, held].astype(f32), axis=2, keepdims=True)
    SB4[:, 0:N] = to_rows(raw.reshape(N, 1))
    s4_s, s4_r = some(8, 8)
    for j in range(1, 8):
        send(lambda: SB4, lambda: SY4.at[y], s4_s + j, s4_r + y, dev(y_=add(y, j, 8)))
    SY4[y] = SB4[...]

    @pl.when(in_half & (zh == 0))
    def _():
        SD[kind_mine, zh] = JP[ym, z]

    recv(GMS, c_s)
    recv(XS, x_s)
    grad_sib = GMS[...]
    for kk in range(2):
        for zz in range(2):
            q = kk * 2 + zz
            part = pl.ds(zz * 4, 4)
            cg[:, q * C : (q + 1) * C] = dot(
                grad_joined, XB[2 * c + kk, part].reshape(N, C), 0, 0
            ) + dot(grad_sib, XS[kk, part].reshape(N, C), 0, 0)

    put(2).start()
    for j in range(1, 8):
        ys = add(y, j, 8)
        recv(SY4.at[ys], s4_r + ys)
    SB5[...] = jnp.sum(SY4[...], axis=0)
    s5_s, s5_r = some(8, 8)
    for j in range(1, 8):
        send(lambda: SB5, lambda: SZ5.at[z], s5_s + j, s5_r + z, dev(z_=add(z, j, 8)))
    SZ5[z] = SB5[...]
    for kind in range(2):
        for zs in range(2):
            z_from = zs * 4 + kind * 2 + yq
            pl.when((z_from != z) | (zh != 0))(lambda: recv(SD.at[kind, zs], k_r + kind * 2 + zs))
    trunk_side = SD[0, 0].astype(f32) + SD[0, 1].astype(f32)
    embed_side = SD[1, 0].astype(f32) + SD[1, 1].astype(f32)
    trunk_normed = trunk * trunk_scale
    embed_normed = embed * embed_scale
    before = GMF[...] + trunk_scale * trunk_side
    PRE[...] = before.astype(bf16)
    o_s, o_r = some(4, 4)
    for j in range(1, 4):
        send(lambda: PRE, lambda: XPR.at[h], o_s + j, o_r + h, dev(h_=add(h, j, 4)))
    XPR[h] = PRE[...]
    for j in range(1, 8):
        zs = add(z, j, 8)
        recv(SZ5.at[zs], s5_r + zs)
    ids = lax.broadcasted_iota(jnp.int32, (8, VC), 0)
    SB7[...] = jnp.where(
        ids == 0,
        (SZ5[0] + SZ5[1] + SZ5[4] + SZ5[5])[0:1],
        jnp.where(ids == 1, (SZ5[2] + SZ5[3] + SZ5[6] + SZ5[7])[0:1], 0.0),
    )
    s7_s, s7_r = some(4, 4)
    for j in range(1, 4):
        send(lambda: SB7, lambda: S7.at[h], s7_s + j, s7_r + h, dev(h_=add(h, j, 4)))
    S7[h] = SB7[...]
    pl.when(owner)(lambda: put(3).start())
    for j in range(1, 4):
        hs = add(h, j, 4)
        recv(S7.at[hs], s7_r + hs)
    INN[...] = to_cols(
        jnp.where(ids == 0, jnp.sum(S7[...], axis=0), S7[h])[:, 0:N]
    ).reshape(4, R, 128)
    dots = INN[zl]
    eg[...] = embed_scale * (embed_side - embed_normed * (embed_scale * pick(dots, 1) / D))
    put(1).start()
    for j in range(1, 4):
        hs = add(h, j, 4)
        recv(XPR.at[hs], o_r + hs)
    tg[...] = jnp.sum(XPR[...].astype(f32), axis=0) - trunk_scale * trunk_normed * (
        trunk_scale * pick(dots, 0) / D
    )

    put(0).start()

    @pl.when(donor)
    def _():
        recv(VSR, q_s)
        ug[...] = VSR[...].astype(f32)
        put(3).start()

    for at in range(4):
        put(at).wait()
    assert counts["r"] <= SEMS
    for cond, body in finals[-POOL:]:
        when(cond, body)


def put_out(*refs):
    into, out, held, sems = refs[:4], refs[4:8], refs[8:12], refs[12]
    reads = [pltpu.make_async_copy(into[k], held[k], sems.at[k]) for k in range(4)]
    writes = [pltpu.make_async_copy(held[k], out[k], sems.at[k + 4]) for k in range(4)]
    order = (2, 3, 0, 1)
    for k in order:
        reads[k].start()
    for k in order:
        reads[k].wait()
        writes[k].start()
    for k in order:
        writes[k].wait()


def local(
    trunk_hidden, next_embeds, combine_weight, final_gain, unembed_weight, target_ids, loss_scale
):
    vm = lambda *shape: pltpu.VMEM(shape, f32)
    vb = lambda *shape: pltpu.VMEM(shape, bf16)
    scratch = [
        vm(R, C), vm(R, C), vm(C, 1280), vm(C, 512),
        vb(2, C, 1280), vb(4, 8, R, C), vb(2, 8, R, C), vm(4, R, CP), vb(4, R, CP), vb(4, R, CP), vm(R, CP),
        vb(8, R, CP), vm(R, C), vb(2, C, V), vm(8, N, VC), vm(8, N, VC), vm(4, R, 128),
        vb(2, N, C), vb(N, C),
        vm(8, VC), vm(8, 8, VC), vm(8, VC), vm(8, 8, VC), vm(8, VC), vm(8, 8, VC),
        vb(8, N, VC), vb(8, N, VC), vm(2, N, C), vb(8, R, C), vb(8, R, C),
        vm(4, R, 128), vm(8, VC), vm(8, 8, VC), vm(8, VC), vm(8, 8, VC),
        vm(N, VC), vm(4, 2, R, 128),
        vm(R, C), vb(4, R, CP), vb(N, C), vb(N, C),
        vb(4, 8, R, C), vb(4, 8, R, C), vb(4, R, C), vb(2, 2, R, C),
        vb(R, C), vb(4, R, C), vm(8, VC), vm(8, 8, VC), vm(8, VC), vm(8, 8, VC),
        vm(8, VC), vm(4, 8, VC),
        vb(4, C, 512), vb(4, C, 512), vb(C, 512), vb(C, 512),
        pltpu.SemaphoreType.DMA((POOL,)), pltpu.SemaphoreType.DMA((SEMS,)), pltpu.SemaphoreType.DMA((6,)),
    ]
    spec = pl.BlockSpec(memory_space=pltpu.VMEM)
    remote = pl.BlockSpec(memory_space=pl.ANY)
    trunk_grad, embed_grad, combine_grad, unembed_grad = pl.pallas_call(
        kernel,
        out_shape=(
            jax.ShapeDtypeStruct((R, C), f32),
            jax.ShapeDtypeStruct((R, C), f32),
            jax.ShapeDtypeStruct((C, 1280), f32),
            jax.ShapeDtypeStruct((C, 512), f32),
        ),
        in_specs=[spec, spec, remote, remote, spec, spec, spec],
        out_specs=(remote,) * 4,
        scratch_shapes=scratch,
        compiler_params=pltpu.CompilerParams(
            collective_id=0, has_side_effects=True, vmem_limit_bytes=60 * 1024 * 1024
        ),
    )(
        trunk_hidden,
        next_embeds[0],
        combine_weight[0].T,
        unembed_weight.T,
        final_gain,
        target_ids,
        loss_scale,
    )
    results = (trunk_grad, embed_grad, combine_grad, unembed_grad)
    trunk_grad, embed_grad, combine_grad, unembed_grad = pl.pallas_call(
        put_out,
        out_shape=tuple(jax.ShapeDtypeStruct(r.shape, r.dtype) for r in results),
        in_specs=[remote] * 4,
        out_specs=(remote,) * 4,
        scratch_shapes=[pltpu.VMEM(r.shape, r.dtype) for r in results]
        + [pltpu.SemaphoreType.DMA((8,))],
        compiler_params=pltpu.CompilerParams(vmem_limit_bytes=60 * 1024 * 1024),
    )(*results)
    return trunk_grad, embed_grad[None], combine_grad.T[None], unembed_grad.T[None, None]


def solution(mesh):
    in_specs = (
        P("dp", "tensor"),
        P("head", "dp", "tensor"),
        P("head", "dp", "tensor"),
        P("tensor"),
        P("dp", "tensor"),
        P("head", None),
        P("head", None),
    )
    out_specs = (
        P("dp", "tensor"),
        P("head", "dp", "tensor"),
        P("head", "dp", "tensor"),
        P("dp", "head", None, "tensor"),
    )
    return jax.shard_map(local, mesh=mesh, in_specs=in_specs, out_specs=out_specs, check_vma=False)
```

```python
import jax
import jax.numpy as jnp
from jax import lax
from jax.experimental import pallas as pl
from jax.experimental.pallas import tpu as pltpu
from jax.sharding import PartitionSpec as P

D = 5120
EPS = 1e-05
R = 48
N = 192
C = 320
CP = 384
V = 2048
VC = 256
MESH = pl.DeviceIdType.MESH
HI = lax.Precision.HIGHEST
POOL = 48
SEMS = 266
f32 = jnp.float32
bf16 = jnp.bfloat16


def dot(left, right, a, b, precision=None):
    return lax.dot_general(
        left, right, (((a,), (b,)), ((), ())), precision=precision, preferred_element_type=f32
    )


def kernel(
    trunk_in, embed_in, w, u, gain, ids_in, scale_in,
    tg_out, eg_out, cg_out, ug_out,
    tg, eg, cg, ug,
    W2, XB, XS, PF, PB, R2, T, Y8, MX, UP, LP, RL, MSC, YN, YS,
    SB0, SY0, SB1, SY1, SB2, SZ2, GA, GS, GN, NB, NR, INN, SB3, SY3, SB6, SZ6, RL2, TW,
    GMF, GMB, GML, GMS, JP, RJ, RJ2, SD, PRE, XPR, SB4, SY4, SB5, S5, VB, VR, VSB, VSR,
    ssem, rsem, lsem,
):
    h = lax.axis_index("head")
    t = lax.axis_index("tensor")
    d = lax.axis_index("dp")
    y, zh = lax.div(t, 2), lax.rem(t, 2)
    zl, c = lax.div(d, 2), lax.rem(d, 2)
    z = zh * 4 + zl
    oc, ozh = 1 - c, 1 - zh

    def dev(h_=None, y_=None, z_=None, c_=None):
        h_ = h if h_ is None else h_
        y_ = y if y_ is None else y_
        z_ = z if z_ is None else z_
        c_ = c if c_ is None else c_
        return (h_, y_ * 2 + lax.div(z_, 4), lax.rem(z_, 4) * 2 + c_)

    def add(value, step, size):
        return lax.rem(value + (step + size), size)

    sib = dev(c_=oc)
    right, left = dev(y_=add(y, 1, 8)), dev(y_=add(y, -1, 8))
    me = dev()

    counts = {"r": 0}

    def slots(n):
        first = counts["r"]
        counts["r"] += n
        return first

    def some(sends, receives):
        return 0, slots(receives)

    finals = []

    def copy(src, dst, s, r, to):
        return pltpu.make_async_remote_copy(
            src_ref=src, dst_ref=dst, send_sem=ssem.at[s], recv_sem=rsem.at[r],
            device_id=to, device_id_type=MESH,
        )

    def when(cond, body):
        if cond is None:
            body()
        else:
            pl.when(cond)(body)

    def send(src, dst, s, r, to, cond=None):
        at = len(finals) % POOL
        if len(finals) >= POOL:
            when(*finals[-POOL])
        when(cond, lambda: copy(src(), dst(), at, r, to).start())
        finals.append((cond, lambda: copy(src(), dst(), at, r, to).wait_send()))

    def recv(dst, r):
        copy(dst, dst, 0, r, me).wait_recv()

    def put(at):
        pairs = ((tg, tg_out), (eg, eg_out), (cg, cg_out), (ug, ug_out))
        return pltpu.make_async_copy(*pairs[at], lsem.at[2 + at])

    lane = lax.broadcasted_iota(jnp.int32, (R, CP), 1)
    e8 = (
        lax.broadcasted_iota(jnp.int32, (8, 128), 0) == lax.broadcasted_iota(jnp.int32, (8, 128), 1)
    ).astype(f32)

    def pick(x, at):
        ids = lax.broadcasted_iota(jnp.int32, x.shape, x.ndim - 1)
        return jnp.sum(jnp.where(ids == at, x, 0.0), axis=-1, keepdims=True)

    def picks(x, at, n):
        ids = lax.broadcasted_iota(jnp.int32, x.shape, x.ndim - 1)
        return jnp.sum(jnp.where((ids >= at) & (ids < at + n), x, 0.0), axis=-1, keepdims=True)

    def in_three(total, at, ids, rest):
        high = total.astype(bf16).astype(f32)
        middle = (total - high).astype(bf16).astype(f32)
        low = total - high - middle
        return jnp.where(
            ids == at, high, jnp.where(ids == at + 1, middle, jnp.where(ids == at + 2, low, rest))
        )

    def to_rows(first, second=None):
        ids = lax.broadcasted_iota(jnp.int32, (first.shape[0], 128), 1)
        v = jnp.where(ids == 0, first, 0.0)
        if second is not None:
            v = jnp.where(ids == 1, second, v)
        return dot(e8, v, 1, 1, HI)

    def to_cols(rows):
        return dot(rows, e8, 0, 0, HI)

    def widen(value, extra):
        T[:, 0:C] = value
        return jnp.where(lane >= C, extra, T[...])

    barrier = pltpu.get_barrier_semaphore()
    peers = [dev(y_=add(y, j, 8)) for j in range(1, 8)]
    peers += [dev(z_=add(z, j, 8)) for j in range(1, 8)]
    peers += [dev(y_=add(y, 4, 8), z_=add(z, j, 8)) for j in range(1, 8)]
    peers += [dev(h_=add(h, i, 4), z_=add(z, j, 8)) for i in range(1, 4) for j in range(8)]
    peers += [sib, dev(z_=ozh * 4 + zl, c_=oc)]
    for to in peers:
        pl.semaphore_signal(barrier, inc=1, device_id=to, device_id_type=MESH)
    own_w = pltpu.make_async_copy(w, W2.at[c], lsem.at[0])
    own_w.start()
    T[...] = jnp.zeros_like(T)
    for ref in (SB0, SB1, SB2, SB3, SB4):
        ref[...] = jnp.zeros_like(ref)
    PF[...] = jnp.zeros_like(PF)
    two = lax.broadcasted_iota(jnp.int32, (8, 384), 0)
    TW[...] = to_cols(
        jnp.where(two == 0, ids_in[...].astype(f32), jnp.where(two == 1, scale_in[...], 0.0))
    ).reshape(4, 2, R, 128)
    chosen = jnp.concatenate([TW[j, c] for j in range(4)], axis=0)
    targets, weights = pick(chosen, 0), pick(chosen, 1)
    pl.semaphore_wait(barrier, len(peers))

    yq, ym = lax.div(y, 4), lax.rem(y, 4)
    hf = lax.rem(zl, 2)
    in_half = hf == yq
    y_to = add(y, 4 * zh, 8)
    first = jnp.where(in_half, 0, 4)
    y_from = hf * 4 + ym
    a_r = slots(4)
    for kind in range(2):
        for zh_to in range(2):
            z_to = zh_to * 4 + kind * 2 + yq
            send(
                lambda kind=kind: (trunk_in, embed_in)[kind], lambda: XB.at[ym, z],
                0, a_r + zl, dev(y_=y_to, z_=z_to), (z_to != z) | (zh != 0),
            )

            def keep(kind=kind):
                XB[ym, z] = (trunk_in, embed_in)[kind][...]

            pl.when((z_to == z) & (zh == 0))(keep)
    w_s = slots(1)
    send(lambda: w, lambda: W2.at[c], w_s, w_s, sib)

    owner = c == zh
    donor = c != zh
    u_f = slots(1)
    u_x, u_q = some(9, 4)
    u_b, u_d = u_x + 4, u_x + 8
    send(lambda: u, lambda: UP.at[zh], u_f, u_f, sib, owner)
    own_u = lambda: pltpu.make_async_copy(u, UP.at[zh], lsem.at[1])
    pl.when(owner)(lambda: own_u().start())

    def quarter_of(at):
        return pl.ds(pl.multiple_of(at * 512, 512), 512)

    mine = quarter_of(h)
    b_s = slots(32)
    for i in range(5):
        for unit in range(4):
            for way in range(2):
                s = add(y, -i, 8) if way == 0 else add(y, i, 8)
                k = lax.rem(s, 4)
                zs = jnp.where(lax.div(s, 4) == hf, 0, 4) + unit
                idx = b_s + (way * 4 + i) * 4 + unit
                if i == 0 and way == 0:
                    pl.when((zs != z) | (zh != 0))(lambda: recv(XB.at[ym, zs], a_r + unit))
                if i > 0 and (i < 4 or unit // 2 == way):
                    recv(XB.at[k, zs], idx - 4)
                if i < 3 or (i == 3 and unit // 2 == way):
                    send(
                        lambda k=k, zs=zs: XB.at[k, zs], lambda k=k, zs=zs: XB.at[k, zs],
                        idx, idx, right if way == 0 else left,
                    )
        if i == 0:
            send(
                lambda: u.at[:, mine], lambda: UP.at[zh, :, mine], u_d, u_q + h,
                dev(z_=ozh * 4 + zl), donor,
            )
        if i == 3:
            pl.when(owner)(lambda: recv(UP.at[ozh, :, mine], u_q + h))
            for j in range(1, 4):
                send(
                    lambda: UP.at[ozh, :, mine], lambda: UP.at[ozh, :, mine], u_x + j, u_q + h,
                    dev(h_=add(h, j, 4)), owner,
                )
            send(lambda: UP.at[ozh, :, mine], lambda: UP.at[ozh, :, mine], u_b, u_q + h, sib, owner)

    own_w.wait()
    recv(W2.at[oc], w_s)
    acc = jnp.zeros((N, C), f32)
    squares = jnp.zeros((N, 1), f32)
    for q in range(8):
        block = XB[q // 2, (q % 2) * 4 : (q % 2) * 4 + 4].reshape(N, C)
        acc = acc + dot(block, W2[q // 4, :, (q % 4) * C : (q % 4 + 1) * C], 1, 1)
        wide = block.astype(f32)
        squares = squares + jnp.sum(wide * wide, axis=1, keepdims=True)
    PF[:, :, 0:C] = acc.reshape(4, R, C)
    lane3 = lax.broadcasted_iota(jnp.int32, (4, R, CP), 2)
    PB[...] = in_three(squares.reshape(4, R, 1), C, lane3, PF[...]).astype(bf16)
    p_s, p_r = some(4, 4)
    for j in range(1, 4):
        zt = add(zl, j, 4)
        send(
            lambda zt=zt: PB.at[zt], lambda: R2.at[zl], p_s + j, p_r + zl, dev(z_=zh * 4 + zt)
        )
    R2[zl] = PB[zl]
    for j in range(1, 4):
        zt = add(zl, j, 4)
        recv(R2.at[zt], p_r + zt)
    from_trunk = R2[0].astype(f32) + R2[1].astype(f32)
    from_embed = R2[2].astype(f32) + R2[3].astype(f32)
    trunk = trunk_in[...].astype(f32)
    embed = embed_in[...].astype(f32)
    trunk_scale = lax.rsqrt(picks(from_trunk, C, 3) / D + EPS)
    embed_scale = lax.rsqrt(picks(from_embed, C, 3) / D + EPS)
    mixed = trunk + trunk_scale * from_trunk[:, 0:C] + embed_scale * from_embed[:, 0:C]
    MX[...] = mixed
    gains = gain[...].reshape(1, C)
    total = jnp.sum(mixed * mixed, axis=1, keepdims=True)
    pieces = in_three(total, C, lane, jnp.zeros((R, CP), f32))
    Y8[z] = widen(mixed * gains, pieces).astype(bf16)
    y_s, y_r = some(8, 8)
    for j in range(1, 8):
        send(lambda: Y8.at[z], lambda: Y8.at[z], y_s + j, y_r + z, dev(z_=add(z, j, 8)))
    for j in range(1, 4):
        ht = add(h, j, 4)
        quarter = quarter_of(ht)
        pl.when(owner)(lambda: recv(UP.at[ozh, :, quarter], u_q + ht))
        send(
            lambda quarter=quarter: UP.at[ozh, :, quarter], lambda quarter=quarter: UP.at[ozh, :, quarter],
            u_b + j, u_q + ht, sib, owner,
        )
    for j in range(1, 8):
        zs = add(z, j, 8)
        recv(Y8.at[zs], y_r + zs)

    x_s = slots(1)
    send(lambda: XB.at[pl.ds(2 * oc, 2)], lambda: XS, x_s, x_s, sib)

    wide = Y8[...].astype(f32)
    split = picks(wide, C, 3)
    part_squares = (split[0:4] + split[4:8]).reshape(N, 1)
    SB0[:, 0:N] = to_rows(part_squares)
    s0_s, s0_r = some(8, 8)
    for j in range(1, 8):
        send(lambda: SB0, lambda: SY0.at[y], s0_s + j, s0_r + y, dev(y_=add(y, j, 8)))
    SY0[y] = SB0[...]

    @pl.when(owner)
    def _():
        own_u().wait()

    @pl.when(donor)
    def _():
        recv(UP.at[zh], u_f)
        for j in range(4):
            recv(UP.at[ozh, :, pl.ds(j * 512, 512)], u_q + j)

    y0 = Y8[0:4].reshape(N, CP)[:, 0:C]
    y1 = Y8[4:8].reshape(N, CP)[:, 0:C]

    def logits_block(at):
        cols = pl.ds(pl.multiple_of(at * VC, VC), VC)
        LP[at] = dot(y0, UP[0, :, cols], 1, 0) + dot(y1, UP[1, :, cols], 1, 0)

    l_s = slots(32)

    def hop(o, way, unit, got):
        to = add(y, o, 8) if way == 0 else add(y, -o, 8)
        rows = slice(unit * R, unit * R + R)
        idx = l_s + (way * 4 + o) * 4 + unit
        if got:
            last = RL2 if (o == 0 and way == 1) else RL.at[to]
            recv(last.at[rows], idx)
            LP[to, rows] = LP[to, rows] + last[rows]
        if o:
            place = RL2 if (o == 1 and way == 1) else RL.at[to]
            send(
                lambda: LP.at[to, rows], lambda: place.at[rows], idx - 4, idx - 4,
                right if way == 0 else left,
            )

    logits_block(add(y, 4, 8))
    for unit in range(2):
        hop(4, 0, unit, False)
        hop(4, 1, unit + 2, False)
    logits_block(add(y, 3, 8))
    logits_block(add(y, -3, 8))
    for unit in range(2):
        hop(3, 0, unit + 2, False)
        hop(3, 1, unit, False)
    logits_block(add(y, 2, 8))
    logits_block(add(y, -2, 8))
    for unit in range(2):
        hop(3, 0, unit, True)
        hop(3, 1, unit + 2, True)
    logits_block(add(y, 1, 8))
    logits_block(add(y, -1, 8))
    logits_block(y)
    for o in (2, 1, 0):
        for unit in (2, 3, 0, 1):
            hop(o, 0, unit, True)
            hop(o, 1, (unit + 2) % 4, True)
    for j in range(1, 8):
        ys = add(y, j, 8)
        recv(SY0.at[ys], s0_r + ys)
    all_squares = to_cols(jnp.sum(SY0[...], axis=0)[:, 0:N])
    mixed_scale = lax.rsqrt(pick(all_squares, 0) / D + EPS)
    MSC[...] = jnp.broadcast_to(mixed_scale, (N, 128)).reshape(4, R, 128)
    YN[0] = (y0.astype(f32) * mixed_scale).astype(bf16)
    YN[1] = (y1.astype(f32) * mixed_scale).astype(bf16)
    n_s = slots(1)
    send(lambda: YN.at[oc], lambda: YS, n_s, n_s, sib)

    logits = LP[y] * mixed_scale
    largest = jnp.max(logits, axis=1, keepdims=True)
    summed = jnp.sum(jnp.exp(logits - largest), axis=1, keepdims=True)
    SB1[:, 0:N] = to_rows(largest, summed)
    s1_s, s1_r = some(8, 8)
    for j in range(1, 8):
        send(lambda: SB1, lambda: SY1.at[y], s1_s + j, s1_r + y, dev(y_=add(y, j, 8)))
    SY1[y] = SB1[...]

    def merge(ref):
        every = ref[...]
        top = jnp.max(every[:, 0:1, :], axis=0)
        whole = jnp.sum(every[:, 1:2, :] * jnp.exp(every[:, 0:1, :] - top[None]), axis=0)
        ids = lax.broadcasted_iota(jnp.int32, (8, VC), 0)
        return jnp.where(ids == 0, top, jnp.where(ids == 1, whole, 0.0))

    for j in range(1, 8):
        ys = add(y, j, 8)
        recv(SY1.at[ys], s1_r + ys)
    SB2[...] = merge(SY1)
    s2_s, s2_r = some(8, 8)
    for j in range(1, 8):
        send(lambda: SB2, lambda: SZ2.at[z], s2_s + j, s2_r + z, dev(z_=add(z, j, 8)))
    SZ2[z] = SB2[...]
    for j in range(1, 8):
        zs = add(z, j, 8)
        recv(SZ2.at[zs], s2_r + zs)
    stats = to_cols(merge(SZ2)[:, 0:N])
    probs = jnp.exp(logits - pick(stats, 0)) / pick(stats, 1)
    vocab_ids = (zl * 4096 + zh * 2048 + y * VC) + lax.broadcasted_iota(jnp.int32, (N, VC), 1)
    hits = (vocab_ids.astype(f32) == targets).astype(f32)
    GA[y] = (weights * (probs - hits)).astype(bf16)

    def normed_block(at, fresh=False):
        rows = pl.ds(pl.multiple_of(at * VC, VC), VC)
        grads = GA[at]
        for zc in range(2):
            value = dot(grads, UP[zc, :, rows], 1, 1)
            GN[zc] = value if fresh else GN[zc] + value

    gs_s = slots(8)

    def to_sibling(at):
        send(lambda: GA.at[at], lambda: GS.at[at], 0, gs_s + at, sib)

    g_s = slots(32)
    for i in range(5):
        for unit in range(4):
            for way in range(2):
                s = add(y, -i, 8) if way == 0 else add(y, i, 8)
                rows = slice(unit * R, unit * R + R)
                idx = g_s + (way * 4 + i) * 4 + unit
                if i > 0 and (i < 4 or unit // 2 == way):
                    recv(GA.at[s, rows], idx - 4)
                if i < 3 or (i == 3 and unit // 2 == way):
                    send(
                        lambda s=s, rows=rows: GA.at[s, rows], lambda s=s, rows=rows: GA.at[s, rows],
                        idx, idx, right if way == 0 else left,
                    )
        arrived = {0: (y,), 4: (add(y, 4, 8),)}.get(i, (add(y, -i, 8), add(y, i, 8)))
        for at in arrived:
            to_sibling(at)
        for at in arrived:
            normed_block(at, i == 0)

    NB[...] = GN[...].astype(bf16).reshape(8, R, C)
    n8_s, n8_r = some(8, 8)
    for j in range(1, 8):
        zt = add(z, j, 8)
        send(lambda zt=zt: NB.at[zt], lambda: NR.at[z], n8_s + j, n8_r + z, dev(z_=zt))
    NR[z] = NB[z]

    held0 = Y8[0:4].reshape(N, CP)[:, 0:C].astype(f32)
    held1 = Y8[4:8].reshape(N, CP)[:, 0:C].astype(f32)
    SB3[:, 0:N] = to_rows(
        jnp.sum(GN[0] * held0, axis=1, keepdims=True) + jnp.sum(GN[1] * held1, axis=1, keepdims=True)
    )
    s3_s, s3_r = some(8, 8)
    for j in range(1, 8):
        send(lambda: SB3, lambda: SY3.at[y], s3_s + j, s3_r + y, dev(y_=add(y, j, 8)))
    SY3[y] = SB3[...]
    for j in range(1, 8):
        ys = add(y, j, 8)
        recv(SY3.at[ys], s3_r + ys)
    SB6[...] = jnp.sum(SY3[...], axis=0)
    s6_s, s6_r = some(8, 8)
    for j in range(1, 8):
        send(lambda: SB6, lambda: SZ6.at[z], s6_s + j, s6_r + z, dev(z_=add(z, j, 8)))
    SZ6[z] = SB6[...]

    for j in range(8):
        recv(GS.at[j], gs_s + j)
    recv(YS, n_s)
    normed_mine = YN[c]
    normed_sib = YS[...]

    def vocab_block(at, carry):
        value = dot(normed_mine, GA[at], 0, 0) + dot(normed_sib, GS[at], 0, 0)
        VB[lax.div(at, 2), :, pl.ds(pl.multiple_of(lax.rem(at, 2) * VC, VC), VC)] = value.astype(bf16)
        return carry

    lax.fori_loop(0, 8, vocab_block, 0)
    v_s, v_r = some(4, 4)
    for j in range(1, 4):
        ht = add(h, j, 4)
        send(lambda ht=ht: VB.at[ht], lambda: VR.at[h], v_s + j, v_r + h, dev(h_=ht))
    VR[h] = VB[h]

    for j in range(1, 8):
        zs = add(z, j, 8)
        recv(NR.at[zs], n8_r + zs)
    scaled = jnp.sum(NR[...].astype(f32), axis=0) * gains
    scale_own = MSC[zl][:, 0:1]
    mixed_normed = MX[...] * scale_own
    for j in range(1, 8):
        zs = add(z, j, 8)
        recv(SZ6.at[zs], s6_r + zs)
    INN[...] = to_cols(jnp.sum(SZ6[...], axis=0)[:, 0:N]).reshape(4, R, 128)
    inner = scale_own * pick(INN[zl], 0)
    grad_mixed = scale_own * (scaled - mixed_normed * (inner / D))
    GMF[...] = grad_mixed
    pieces = in_three(trunk_scale, C, lane, in_three(embed_scale, C + 3, lane, jnp.zeros((R, CP), f32)))
    GMB[zl] = widen(grad_mixed, pieces).astype(bf16)
    d_s, d_r = some(4, 4)
    for j in range(1, 4):
        zt = add(zl, j, 4)
        send(lambda: GMB.at[zl], lambda: GMB.at[zl], d_s + j, d_r + zl, dev(z_=zh * 4 + zt))

    for j in range(1, 4):
        zs = add(zl, j, 4)
        recv(GMB.at[zs], d_r + zs)
    gathered = GMB[...].reshape(N, CP)
    grad_low = gathered[:, 0:C]
    joined_scale = picks(gathered.astype(f32), C + 3 * lax.div(zl, 2), 3)
    grad_joined = (grad_low.astype(f32) * joined_scale).astype(bf16)
    GML[...] = grad_joined
    c_s = slots(1)
    send(lambda: GML, lambda: GMS, c_s, c_s, sib)

    for q in range(8):
        value = dot(grad_low, W2[q // 4, :, (q % 4) * C : (q % 4 + 1) * C], 1, 0)
        JP[q // 2, (q % 2) * 4 : (q % 2) * 4 + 4] = value.astype(bf16).reshape(4, R, C)
    q_s = slots(1)

    def sum_vocab():
        for j in range(1, 4):
            hs = add(h, j, 4)
            recv(VR.at[hs], v_r + hs)
        vocab_total = jnp.sum(VR[...].astype(f32), axis=0)
        ug[...] = vocab_total
        VSB[...] = vocab_total.astype(bf16)
        send(lambda: VSB, lambda: VSR, q_s, q_s, dev(z_=ozh * 4 + zl, c_=oc), donor)

    j_s = slots(32)

    def grad_hop(o, way, unit, got):
        to = add(y, o, 8) if way == 0 else add(y, -o, 8)
        k = lax.rem(to, 4)
        part = jnp.where(lax.div(to, 4) == hf, 0, 4) + unit
        idx = j_s + (way * 4 + o) * 4 + unit
        if got:
            last = RJ2.at[unit] if (o == 0 and way == 1) else RJ.at[k, part]
            recv(last, idx)
            JP[k, part] = (JP[k, part].astype(f32) + last[...].astype(f32)).astype(bf16)
        if o:
            place = RJ2.at[unit] if (o == 1 and way == 1) else RJ.at[k, part]
            send(
                lambda: JP.at[k, part], lambda: place, idx - 4, idx - 4,
                right if way == 0 else left,
            )

    for unit in range(2):
        grad_hop(4, 0, unit, False)
        grad_hop(4, 1, unit + 2, False)
    for unit in range(2):
        grad_hop(3, 0, unit + 2, False)
        grad_hop(3, 1, unit, False)
    for unit in range(2):
        grad_hop(3, 0, unit, True)
        grad_hop(3, 1, unit + 2, True)
    for o in (2, 1, 0):
        for unit in (2, 3, 0, 1):
            grad_hop(o, 0, unit, True)
            grad_hop(o, 1, (unit + 2) % 4, True)
        if o == 2:
            sum_vocab()
    kind_mine = lax.div(zl, 2)
    k_r = slots(4)
    for part in range(4):
        z_to = first + part
        send(
            lambda z_to=z_to: JP.at[ym, z_to], lambda: SD.at[kind_mine, zh], 0,
            k_r + kind_mine * 2 + zh, dev(y_=y_from, z_=z_to), jnp.logical_not(in_half & (z_to == z)),
        )

    held = pl.ds(first, 4)
    raw = jnp.sum(JP[ym, held].astype(f32) * XB[ym, held].astype(f32), axis=2, keepdims=True)
    SB4[:, 0:N] = to_rows(raw.reshape(N, 1))
    s4_s, s4_r = some(8, 8)
    for j in range(1, 8):
        send(lambda: SB4, lambda: SY4.at[y], s4_s + j, s4_r + y, dev(y_=add(y, j, 8)))
    SY4[y] = SB4[...]

    @pl.when(in_half & (zh == 0))
    def _():
        SD[kind_mine, zh] = JP[ym, z]

    recv(GMS, c_s)
    recv(XS, x_s)
    grad_sib = GMS[...]
    for kk in range(2):
        for zz in range(2):
            q = kk * 2 + zz
            part = pl.ds(zz * 4, 4)
            cg[:, q * C : (q + 1) * C] = dot(
                grad_joined, XB[2 * c + kk, part].reshape(N, C), 0, 0
            ) + dot(grad_sib, XS[kk, part].reshape(N, C), 0, 0)

    put(2).start()
    for j in range(1, 8):
        ys = add(y, j, 8)
        recv(SY4.at[ys], s4_r + ys)
    SB5[...] = jnp.sum(SY4[...], axis=0)
    s5_r = slots(32)
    for i in range(4):
        for j in range(8):
            if i + j:
                send(
                    lambda: SB5, lambda: S5.at[h, z], 0, s5_r + h * 8 + z,
                    dev(h_=add(h, i, 4), z_=add(z, j, 8)), zl < 2 if i else None,
                )
    S5[h, z] = SB5[...]
    for kind in range(2):
        for zs in range(2):
            z_from = zs * 4 + kind * 2 + yq
            pl.when((z_from != z) | (zh != 0))(lambda: recv(SD.at[kind, zs], k_r + kind * 2 + zs))
    trunk_side = SD[0, 0].astype(f32) + SD[0, 1].astype(f32)
    embed_side = SD[1, 0].astype(f32) + SD[1, 1].astype(f32)
    trunk_normed = trunk * trunk_scale
    embed_normed = embed * embed_scale
    before = GMF[...] + trunk_scale * trunk_side
    PRE[...] = before.astype(bf16)
    o_s, o_r = some(4, 4)
    for j in range(1, 4):
        send(lambda: PRE, lambda: XPR.at[h], o_s + j, o_r + h, dev(h_=add(h, j, 4)))
    XPR[h] = PRE[...]
    pl.when(owner)(lambda: put(3).start())
    for i in range(4):
        for j in range(8):
            if i + j:
                hs, zs = add(h, i, 4), add(z, j, 8)
                when(
                    lax.rem(zs, 4) < 2 if i else None,
                    lambda: recv(S5.at[hs, zs], s5_r + hs * 8 + zs),
                )
    ids = lax.broadcasted_iota(jnp.int32, (8, VC), 0)
    of_trunk = jnp.sum(S5[:, 0] + S5[:, 1] + S5[:, 4] + S5[:, 5], axis=0)[0:1]
    of_embed = (S5[h, 2] + S5[h, 3] + S5[h, 6] + S5[h, 7])[0:1]
    INN[...] = to_cols(
        jnp.where(ids == 0, of_trunk, jnp.where(ids == 1, of_embed, 0.0))[:, 0:N]
    ).reshape(4, R, 128)
    dots = INN[zl]
    eg[...] = embed_scale * (embed_side - embed_normed * (embed_scale * pick(dots, 1) / D))
    put(1).start()
    for j in range(1, 4):
        hs = add(h, j, 4)
        recv(XPR.at[hs], o_r + hs)
    tg[...] = jnp.sum(XPR[...].astype(f32), axis=0) - trunk_scale * trunk_normed * (
        trunk_scale * pick(dots, 0) / D
    )

    put(0).start()

    @pl.when(donor)
    def _():
        recv(VSR, q_s)
        ug[...] = VSR[...].astype(f32)
        put(3).start()

    for at in range(4):
        put(at).wait()
    assert counts["r"] <= SEMS
    for cond, body in finals[-POOL:]:
        when(cond, body)


def put_out(*refs):
    into, out, held, sems = refs[:4], refs[4:8], refs[8:12], refs[12]
    parts = [(2, slice(80 * n, 80 * n + 80)) for n in range(4)]
    parts += [(3, slice(0, 160)), (3, slice(160, 320)), (0, slice(0, R)), (1, slice(0, R))]

    def move(n, ins):
        k, rows = parts[n]
        source, target = (into, held) if ins else (held, out)
        return pltpu.make_async_copy(
            source[k].at[rows], target[k].at[rows], sems.at[n + (0 if ins else 8)]
        )

    for n in range(8):
        move(n, True).start()
    for n in range(8):
        move(n, True).wait()
        move(n, False).start()
    for n in range(8):
        move(n, False).wait()


def local(
    trunk_hidden, next_embeds, combine_weight, final_gain, unembed_weight, target_ids, loss_scale
):
    vm = lambda *shape: pltpu.VMEM(shape, f32)
    vb = lambda *shape: pltpu.VMEM(shape, bf16)
    scratch = [
        vm(R, C), vm(R, C), vm(C, 1280), vm(C, 512),
        vb(2, C, 1280), vb(4, 8, R, C), vb(2, 8, R, C), vm(4, R, CP), vb(4, R, CP), vb(4, R, CP), vm(R, CP),
        vb(8, R, CP), vm(R, C), vb(2, C, V), vm(8, N, VC), vm(8, N, VC), vm(4, R, 128),
        vb(2, N, C), vb(N, C),
        vm(8, VC), vm(8, 8, VC), vm(8, VC), vm(8, 8, VC), vm(8, VC), vm(8, 8, VC),
        vb(8, N, VC), vb(8, N, VC), vm(2, N, C), vb(8, R, C), vb(8, R, C),
        vm(4, R, 128), vm(8, VC), vm(8, 8, VC), vm(8, VC), vm(8, 8, VC),
        vm(N, VC), vm(4, 2, R, 128),
        vm(R, C), vb(4, R, CP), vb(N, C), vb(N, C),
        vb(4, 8, R, C), vb(4, 8, R, C), vb(4, R, C), vb(2, 2, R, C),
        vb(R, C), vb(4, R, C), vm(8, VC), vm(8, 8, VC), vm(8, VC), vm(4, 8, 8, VC),
        vb(4, C, 512), vb(4, C, 512), vb(C, 512), vb(C, 512),
        pltpu.SemaphoreType.DMA((POOL,)), pltpu.SemaphoreType.DMA((SEMS,)), pltpu.SemaphoreType.DMA((6,)),
    ]
    spec = pl.BlockSpec(memory_space=pltpu.VMEM)
    remote = pl.BlockSpec(memory_space=pl.ANY)
    trunk_grad, embed_grad, combine_grad, unembed_grad = pl.pallas_call(
        kernel,
        out_shape=(
            jax.ShapeDtypeStruct((R, C), f32),
            jax.ShapeDtypeStruct((R, C), f32),
            jax.ShapeDtypeStruct((C, 1280), f32),
            jax.ShapeDtypeStruct((C, 512), f32),
        ),
        in_specs=[spec, spec, remote, remote, spec, spec, spec],
        out_specs=(remote,) * 4,
        scratch_shapes=scratch,
        compiler_params=pltpu.CompilerParams(
            collective_id=0, has_side_effects=True, vmem_limit_bytes=60 * 1024 * 1024
        ),
    )(
        trunk_hidden,
        next_embeds[0],
        combine_weight[0].T,
        unembed_weight.T,
        final_gain,
        target_ids,
        loss_scale,
    )
    results = (trunk_grad, embed_grad, combine_grad, unembed_grad)
    trunk_grad, embed_grad, combine_grad, unembed_grad = pl.pallas_call(
        put_out,
        out_shape=tuple(jax.ShapeDtypeStruct(r.shape, r.dtype) for r in results),
        in_specs=[remote] * 4,
        out_specs=(remote,) * 4,
        scratch_shapes=[pltpu.VMEM(r.shape, r.dtype) for r in results]
        + [pltpu.SemaphoreType.DMA((16,))],
        compiler_params=pltpu.CompilerParams(vmem_limit_bytes=60 * 1024 * 1024),
    )(*results)
    return trunk_grad, embed_grad[None], combine_grad.T[None], unembed_grad.T[None, None]


def solution(mesh):
    in_specs = (
        P("dp", "tensor"),
        P("head", "dp", "tensor"),
        P("head", "dp", "tensor"),
        P("tensor"),
        P("dp", "tensor"),
        P("head", None),
        P("head", None),
    )
    out_specs = (
        P("dp", "tensor"),
        P("head", "dp", "tensor"),
        P("head", "dp", "tensor"),
        P("dp", "head", None, "tensor"),
    )
    return jax.shard_map(local, mesh=mesh, in_specs=in_specs, out_specs=out_specs, check_vma=False)
```
